512 devices in a mesh: context: 64 (over y, z), channel: 8 (over x, core).
Axes of the slice: x: 4, y: 8, z: 8, core: 2. Of those that a mesh axis runs over, the one named last changes fastest.
Arguments:
- inputs: bfloat16 [512, 32768], P('channel', 'context'), may hold values from -6 to 6
- grad_out: bfloat16 [512, 32768], P('channel', 'context'), may hold values from -36 to 36
- decay_rates: float32 [64, 16], replicated, as said below
- residues: float32 [64, 16], replicated, may hold values from -1.5 to 1.5
Outputs:
- grad_in: bfloat16 [512, 32768], P('channel', 'context')
- grad_residue: float32 [64, 16], replicated
- grad_log_rate: float32 [64, 16], replicated
The draws below stay inside these ranges and needn't reach their ends.
Inputs may be any that keep to these rules, and one draw needn't show every extreme that they name: `decay_rates`: every rate lies between 0.3 / 32768 and 1 / 15.
All inputs are finite; a program needn't handle non-finite values.
Results may differ from the reference program's by a relative error of at most 0.001.
Values may be sent and summed in bfloat16 or wider, within the bound.
No kernel may reach another device: no remote copies, remote signals or barrier semaphores. Data moves between devices by JAX's collectives and lax.ppermute only.
A program may use at most 64 MiB of HBM per device.

```python
import math
import jax
import jax.numpy as jnp
from jax import lax

ORDER = 16
CHANNELS = 512
FILTERS = 64
GROUP = 8
SEQ = 32768


def draw_decay_rates(key, part):
    key_pick, key_level = jax.random.split(key)
    slow_share = 0.5
    slow_pick = jax.random.bernoulli(key_pick, slow_share, (FILTERS, ORDER))
    level = jax.random.uniform(key_level, (FILTERS, ORDER), jnp.float32)
    lowest = math.log(0.3 / SEQ)
    middle = math.log(2.3 / SEQ)
    highest = math.log(1.0 / 15.0)
    slow_rate = jnp.exp(lowest + level * (middle - lowest))
    fast_rate = jnp.exp(middle + level * (highest - middle))
    return jnp.where(slow_pick, slow_rate, fast_rate).astype(jnp.float32)


def draw_grad_out(key, part):
    primary_key = jax.random.fold_in(key, 0)
    along_seq = 1.0 + 2.0 * jnp.arange(SEQ, dtype=jnp.float32) / SEQ
    member = (jnp.arange(CHANNELS) // FILTERS).astype(jnp.float32)
    across = 1.0 + 2.0 * member / max(GROUP - 1, 1)
    scale_factor = across[:, None] * along_seq[None, :]
    values = jnp.clip(jax.random.normal(primary_key, (CHANNELS, SEQ), jnp.float32), -4.0, 4.0)
    return (values * scale_factor).astype(jnp.bfloat16)


def block_scale(stream_key, shape, shards, low, high):
    factor_of = 1.0
    for axis_at, shards_of in shards:
        heights = jax.random.uniform(jax.random.fold_in(jax.random.fold_in(stream_key, 6), axis_at), (shards_of,), jnp.float32, low / len(shards), high / len(shards))
        factor_of = factor_of * jnp.repeat(jnp.exp(heights), shape[axis_at] // shards_of).reshape((-1,) + (1,) * (len(shape) - 1 - axis_at))
    return factor_of


def scatter_about(rng, dims, deviation, limit, cuts=(), held_as=jnp.bfloat16):
    array = deviation * jax.random.normal(rng, dims, jnp.float32)
    if cuts:
        array = array * block_scale(rng, dims, cuts, -0.22, 0.18)
    return jnp.clip(array, -limit, limit).astype(held_as)


def setup_inputs(seed: int = 0) -> dict:
    streams_of = jax.random.split(jax.random.key(seed), 5)
    return {
        "inputs": scatter_about(streams_of[0], (CHANNELS, SEQ), 1.0, 6.0, ((0, 8), (1, 64))),
        "grad_out": draw_grad_out(jax.random.fold_in(streams_of[4], 71), 0),
        "decay_rates": draw_decay_rates(jax.random.fold_in(streams_of[4], 71), 0),
        "residues": scatter_about(streams_of[3], (FILTERS, ORDER), 0.25, 1.5, (), jnp.float32),
    }


precise_setting = lax.Precision.HIGHEST

def reference(inputs, grad_out, decay_rates, residues):
    chan_total, seq_total = inputs.shape
    filter_count = decay_rates.shape[0]
    group_size = chan_total // filter_count
    gain_pole = jnp.sqrt(-jnp.expm1(-2.0 * decay_rates))
    decay_step = jnp.exp(-decay_rates)
    weighted = residues * gain_pole
    lag_values = jnp.arange(seq_total, dtype=jnp.float32)

    def taps_row(operands):
        rate_row, weight_row = operands
        return jnp.dot(weight_row, jnp.exp(-rate_row[:, None] * lag_values[None, :]), precision=precise_setting)
    filter_taps = lax.map(taps_row, (decay_rates, weighted))
    fft_size = 2 * seq_total
    taps_freq = jnp.fft.rfft(filter_taps, fft_size, axis=1)

    def one_group(operands):
        x_group, g_group = operands
        x_freq = jnp.fft.rfft(x_group.astype(jnp.float32), fft_size, axis=1)
        g_freq = jnp.fft.rfft(g_group.astype(jnp.float32), fft_size, axis=1)
        back_conv = jnp.fft.irfft(jnp.conj(taps_freq) * g_freq, fft_size, axis=1)[:, :seq_total]
        cross_corr = jnp.fft.irfft(g_freq * jnp.conj(x_freq), fft_size, axis=1)[:, :seq_total]
        return (back_conv.astype(jnp.bfloat16), cross_corr)
    grad_parts, cross_parts = lax.map(one_group, (inputs.reshape(group_size, filter_count, seq_total), grad_out.reshape(group_size, filter_count, seq_total)))
    grad_in = grad_parts.reshape(chan_total, seq_total)
    corr_total = lax.optimization_barrier(jnp.sum(cross_parts, axis=0))

    def project_row(operands):
        rate_row, corr_row = operands
        powers = jnp.exp(-rate_row[:, None] * lag_values[None, :])
        return (jnp.dot(powers, corr_row, precision=precise_setting), jnp.dot(powers, corr_row * lag_values, precision=precise_setting))
    first_sum, second_sum = lax.map(project_row, (decay_rates, corr_total))
    norm_scale = 1.0 / math.sqrt(seq_total * group_size)
    grad_residue = gain_pole * first_sum * norm_scale
    grad_log_rate = residues * decay_rates * (decay_step * decay_step / gain_pole * first_sum - gain_pole * second_sum) * norm_scale
    return (grad_in, grad_residue, grad_log_rate)
```

```python
import functools
import math

import jax
import jax.numpy as jnp
from jax import lax
from jax.experimental import pallas as pl
from jax.experimental.pallas import tpu as pltpu
from jax.sharding import PartitionSpec as P

LANES = 128
SUBLANES = 8
CHANNELS = 64
POLES = 16
STEP = 32
HALF = SUBLANES * STEP
CHUNK = 2 * HALF
ROWS = 8
GROUP = 8


def low_half(shape):
    return lax.broadcasted_iota(jnp.int32, shape, len(shape) - 1) < CHANNELS


def double(rows):
    return jnp.concatenate([rows, rows], axis=1)


def pack(ref):
    even = ref[pl.ds(0, SUBLANES, stride=2), :]
    odd = ref[pl.ds(1, SUBLANES, stride=2), :]
    return jnp.where(low_half(even.shape), even, odd)


def transposed(block):
    stacked = jnp.concatenate([block[:, :HALF], block[:, HALF:]], axis=0)
    return stacked.astype(jnp.float32).T


def pre_kernel(x_ref, g_ref, rate_ref, msg_ref, ain_ref, gt_ref, xt_ref, rate2_ref, rows_ref, blk_ref):
    gt_ref[...] = transposed(g_ref[...])
    xt_ref[...] = transposed(x_ref[...])
    rate2_ref[...] = double(rate_ref[...])
    full = (SUBLANES, LANES)
    low = low_half(full)
    block = lax.broadcasted_iota(jnp.int32, full, 0)
    after = (SUBLANES - 1 - block).astype(jnp.float32)
    after_all = jnp.where(low, after + SUBLANES, after)
    zero = jnp.zeros(full, jnp.float32)
    for first in range(0, POLES, 8):
        poles = range(first, first + 8)
        decay = [jnp.broadcast_to(jnp.exp(-rate2_ref[pl.ds(k, 1), :]), full) for k in poles]
        total = [zero] * 8
        slope = [zero] * 8
        value = [zero] * 8
        tilt = [zero] * 8
        for j in reversed(range(STEP)):
            g = gt_ref[pl.ds(j, SUBLANES, stride=STEP), :]
            x = xt_ref[pl.ds(j, SUBLANES, stride=STEP), :]
            for i in range(8):
                slope[i] = decay[i] * (slope[i] + total[i])
                total[i] = decay[i] * total[i] + g
                value[i] = value[i] + x * total[i]
                tilt[i] = tilt[i] + x * slope[i]
        for i, k in enumerate(poles):
            blk_ref[0, k] = total[i]
            blk_ref[1, k] = slope[i]
            blk_ref[2, k] = value[i]
            blk_ref[3, k] = tilt[i]
        state = [zero] * 8
        lean = [zero] * 8
        for j in range(STEP):
            x = xt_ref[pl.ds(j, SUBLANES, stride=STEP), :]
            for i in range(8):
                state[i] = decay[i] * (state[i] + x)
                lean[i] = decay[i] * lean[i] + state[i]
        for i, k in enumerate(poles):
            blk_ref[4, k] = state[i]
            blk_ref[5, k] = lean[i]
    for k in range(POLES):
        rate = rate2_ref[pl.ds(k, 1), :]
        total, slope = blk_ref[0, k], blk_ref[1, k]
        state, lean = blk_ref[4, k], blk_ref[5, k]
        for shift in (1, 2, 4):
            far = jnp.where(block < SUBLANES - shift, jnp.exp(-(STEP * shift) * rate), 0.0)
            moved = pltpu.roll(total, SUBLANES - shift, 0)
            turned = pltpu.roll(slope, SUBLANES - shift, 0)
            slope = slope + far * (turned + float(STEP * shift) * moved)
            total = total + far * moved
        rows_ref[0, pl.ds(k, 1), :] = total[0:1]
        rows_ref[1, pl.ds(k, 1), :] = slope[0:1]
        inside = block < SUBLANES - 1
        moved = jnp.where(inside, pltpu.roll(total, SUBLANES - 1, 0), 0.0)
        turned = jnp.where(inside, pltpu.roll(slope, SUBLANES - 1, 0), 0.0)
        late = jnp.where(low, pltpu.roll(jnp.broadcast_to(total[0:1], full), CHANNELS, 1), 0.0)
        late_slope = jnp.where(low, pltpu.roll(jnp.broadcast_to(slope[0:1], full), CHANNELS, 1), 0.0)
        reach = jnp.exp(-(float(STEP) * after) * rate)
        coming = moved + reach * late
        coming_slope = turned + reach * (late_slope + (float(STEP) * after) * late)
        ain_ref[k] = coming
        value = blk_ref[2, k] + state * coming
        tilt = blk_ref[3, k] + lean * coming + state * coming_slope
        away = float(STEP) * after_all
        weight = jnp.exp(-away * rate)
        rows_ref[2, pl.ds(k, 1), :] = jnp.sum(weight * state, axis=0, keepdims=True)
        rows_ref[3, pl.ds(k, 1), :] = jnp.sum(weight * (lean + away * state), axis=0, keepdims=True)
        rows_ref[4, pl.ds(k, 1), :] = jnp.sum(value, axis=0, keepdims=True)
        rows_ref[5, pl.ds(k, 1), :] = jnp.sum(tilt, axis=0, keepdims=True)
    rates = rate2_ref[...]
    low_rows = low_half(rates.shape)
    jump = jnp.where(low_rows, 1.0, jnp.exp(-float(HALF) * rates))
    length = jnp.where(low_rows, 0.0, float(HALF))
    rows_ref[1] = jump * (rows_ref[1] + length * rows_ref[0])
    rows_ref[0] = jump * rows_ref[0]
    for q in range(6):
        both = rows_ref[q] + pltpu.roll(rows_ref[q], CHANNELS, 1)
        rows_ref[q] = both
        packed = pack(rows_ref.at[q])
        for d in range(ROWS):
            msg_ref[d, pl.ds(q * SUBLANES, SUBLANES), :] = packed


def combine(recv_ref, rate, span):
    part = lambda d, q: recv_ref[d, pl.ds(q * SUBLANES, SUBLANES), :]
    decay = jnp.exp(-span * rate)
    coming = jnp.zeros_like(rate)
    coming_slope = jnp.zeros_like(rate)
    value = part(ROWS - 1, 4)
    tilt = part(ROWS - 1, 5)
    arriving = [coming] * ROWS
    for d in reversed(range(ROWS - 1)):
        coming_slope = part(d + 1, 1) + decay * (coming_slope + span * coming)
        coming = part(d + 1, 0) + decay * coming
        arriving[d] = coming
        value = value + part(d, 4) + part(d, 2) * coming
        tilt = tilt + part(d, 5) + part(d, 3) * coming + part(d, 2) * coming_slope
    slope = part(0, 1) + decay * (coming_slope + span * coming)
    total = part(0, 0) + decay * coming
    state = part(0, 2)
    lean = part(0, 3)
    for d in range(1, ROWS):
        lean = part(d, 3) + decay * (lean + span * state)
        state = part(d, 2) + decay * state
    return total, slope, state, lean, value, tilt, arriving


def pick(at, choices):
    out = choices[0]
    for d in range(1, ROWS):
        out = jnp.where(at == d, choices[d], out)
    return out


def row_kernel(at_ref, recv_ref, rate_ref, msg_ref, arrive_ref, rate2_ref):
    rate2_ref[...] = double(rate_ref[...])
    rate = pack(rate2_ref)
    *sums, arriving = combine(recv_ref, rate, float(CHUNK))
    for q, packed in enumerate(sums):
        for d in range(ROWS):
            msg_ref[d, pl.ds(q * SUBLANES, SUBLANES), :] = packed
    arrive_ref[...] = pick(at_ref[0], arriving)


def column_kernel(at_ref, recv_ref, rate_ref, arrive_ref, msg_ref, state_ref, rate2_ref):
    rate2_ref[...] = double(rate_ref[...])
    rate = pack(rate2_ref)
    sums = combine(recv_ref, rate, float(CHUNK * ROWS))
    for q in range(2):
        for d in range(GROUP):
            msg_ref[d, pl.ds(q * SUBLANES, SUBLANES), :] = sums[4 + q]
    after = float(CHUNK) * (ROWS - 1 - at_ref[0]).astype(jnp.float32)
    state_ref[...] = arrive_ref[...] + jnp.exp(-after * rate) * pick(at_ref[1], sums[6])


def post_kernel(g_ref, rate_ref, weight_ref, ain_ref, state_ref, out_ref, gt_ref, yt_ref, rate2_ref, weight2_ref):
    gt_ref[...] = transposed(g_ref[...])
    rate2_ref[...] = double(rate_ref[...])
    weight2_ref[...] = double(weight_ref[...])
    full = (SUBLANES, LANES)
    low = low_half(full)
    low_row = low_half((1, LANES))
    after = (SUBLANES - 1 - lax.broadcasted_iota(jnp.int32, full, 0)).astype(jnp.float32)
    away = float(STEP) * jnp.where(low, after + SUBLANES, after)
    for first in range(0, POLES, 8):
        poles = range(first, first + 8)
        decay = [jnp.broadcast_to(jnp.exp(-rate2_ref[pl.ds(k, 1), :]), full) for k in poles]
        weight = [jnp.broadcast_to(weight2_ref[pl.ds(k, 1), :], full) for k in poles]
        total = []
        for k in poles:
            row = state_ref[pl.ds(k // 2, 1), :]
            other = pltpu.roll(row, CHANNELS, 1)
            both = jnp.where(low_row, row, other) if k % 2 == 0 else jnp.where(low_row, other, row)
            total.append(ain_ref[k] + jnp.exp(-away * rate2_ref[pl.ds(k, 1), :]) * both)
        for j in reversed(range(STEP)):
            at = pl.ds(j, SUBLANES, stride=STEP)
            g = gt_ref[at, :]
            for i in range(8):
                total[i] = decay[i] * total[i] + g
            terms = [weight[i] * total[i] for i in range(8)]
            while len(terms) > 1:
                terms = [terms[i] + terms[i + 1] for i in range(0, len(terms), 2)]
            yt_ref[at, :] = terms[0] if first == 0 else yt_ref[at, :] + terms[0]
    stacked = yt_ref[...].T
    out_ref[:, :HALF] = stacked[:CHANNELS].astype(jnp.bfloat16)
    out_ref[:, HALF:] = stacked[CHANNELS:].astype(jnp.bfloat16)


def final_kernel(recv_ref, one_ref, two_ref, three_ref, res_ref, log_ref):
    value = recv_ref[0, pl.ds(0, SUBLANES), :]
    tilt = recv_ref[0, pl.ds(SUBLANES, SUBLANES), :]
    for d in range(1, GROUP):
        value = value + recv_ref[d, pl.ds(0, SUBLANES), :]
        tilt = tilt + recv_ref[d, pl.ds(SUBLANES, SUBLANES), :]
    for k in range(POLES):
        lanes = slice(0, CHANNELS) if k % 2 == 0 else slice(CHANNELS, LANES)
        first = value[k // 2 : k // 2 + 1, lanes]
        second = tilt[k // 2 : k // 2 + 1, lanes]
        at = pl.ds(k, 1)
        res_ref[at, :] = one_ref[at, :] * first
        log_ref[at, :] = two_ref[at, :] * first - three_ref[at, :] * second


def vmem(count):
    return [pl.BlockSpec(memory_space=pltpu.VMEM)] * count


def f32(*shape):
    return jax.ShapeDtypeStruct(shape, jnp.float32)


def scratch(*shape):
    return pltpu.VMEM(shape, jnp.float32)


def body(inputs, grad_out, decay_rates, residues):
    rate = decay_rates.T
    residue = residues.T
    place = lax.axis_index("context")
    at = jnp.stack([place % ROWS, place // ROWS]).astype(jnp.int32)
    rows = [[y * ROWS + z for z in range(ROWS)] for y in range(ROWS)]
    columns = [[y * ROWS + z for y in range(ROWS)] for z in range(ROWS)]
    smem = [pl.BlockSpec(memory_space=pltpu.SMEM)]

    message, coming = pl.pallas_call(
        pre_kernel,
        out_shape=(f32(ROWS, 6 * SUBLANES, LANES), f32(POLES, SUBLANES, LANES)),
        in_specs=vmem(3),
        out_specs=tuple(vmem(2)),
        scratch_shapes=[
            scratch(HALF, LANES),
            scratch(HALF, LANES),
            scratch(POLES, LANES),
            scratch(6, POLES, LANES),
            scratch(6, POLES, SUBLANES, LANES),
        ],
        name="pre",
    )(inputs, grad_out, rate)
    received = lax.all_to_all(message, "context", 0, 0, axis_index_groups=rows, tiled=True)
    message, arrived = pl.pallas_call(
        row_kernel,
        out_shape=(f32(ROWS, 6 * SUBLANES, LANES), f32(SUBLANES, LANES)),
        in_specs=smem + vmem(2),
        out_specs=tuple(vmem(2)),
        scratch_shapes=[scratch(POLES, LANES)],
        name="row",
    )(at, received, rate)
    received = lax.all_to_all(message, "context", 0, 0, axis_index_groups=columns, tiled=True)
    message, state = pl.pallas_call(
        column_kernel,
        out_shape=(f32(GROUP, 2 * SUBLANES, LANES), f32(SUBLANES, LANES)),
        in_specs=smem + vmem(3),
        out_specs=tuple(vmem(2)),
        scratch_shapes=[scratch(POLES, LANES)],
        name="column",
    )(at, received, rate, arrived)
    received = lax.all_to_all(message, "channel", 0, 0, tiled=True)

    gain = jnp.sqrt(-jnp.expm1(-2.0 * rate))
    decay = jnp.exp(-rate)
    grad_in = pl.pallas_call(
        post_kernel,
        out_shape=jax.ShapeDtypeStruct((CHANNELS, CHUNK), jnp.bfloat16),
        in_specs=vmem(5),
        out_specs=vmem(1)[0],
        scratch_shapes=[scratch(HALF, LANES), scratch(HALF, LANES), scratch(POLES, LANES), scratch(POLES, LANES)],
        name="post",
    )(grad_out, rate, residue * gain, coming, state)
    norm = 1.0 / math.sqrt(CHUNK * ROWS * ROWS * GROUP)
    scaled = residue * rate * norm
    res_grad, log_grad = pl.pallas_call(
        final_kernel,
        out_shape=(f32(POLES, CHANNELS), f32(POLES, CHANNELS)),
        in_specs=vmem(4),
        out_specs=tuple(vmem(2)),
        name="final",
    )(received, gain * norm, scaled * (decay * decay / gain), scaled * gain)
    return (grad_in, res_grad.T, log_grad.T)


def solution(mesh):
    return jax.shard_map(
        body,
        mesh=mesh,
        in_specs=(P("channel", "context"), P("channel", "context"), P(), P()),
        out_specs=(P("channel", "context"), P(), P()),
        check_vma=False,
    )
```

```python
import functools
import math

import jax
import jax.numpy as jnp
from jax import lax
from jax.experimental import pallas as pl
from jax.experimental.pallas import tpu as pltpu
from jax.sharding import PartitionSpec as P

LANES = 128
SUBLANES = 8
CHANNELS = 64
POLES = 16
STEP = 32
HALF = SUBLANES * STEP
CHUNK = 2 * HALF
ROWS = 8
GROUP = 8
GRANT = pltpu.CompilerParams(vmem_limit_bytes=8 << 20)


def low_half(shape):
    return lax.broadcasted_iota(jnp.int32, shape, len(shape) - 1) < CHANNELS


def double(rows):
    return jnp.concatenate([rows, rows], axis=1)


def pack(ref):
    even = ref[pl.ds(0, SUBLANES, stride=2), :]
    odd = ref[pl.ds(1, SUBLANES, stride=2), :]
    return jnp.where(low_half(even.shape), even, odd)


def transposed(block):
    stacked = jnp.concatenate([block[:, :HALF], block[:, HALF:]], axis=0)
    return stacked.astype(jnp.float32).T


def pre_kernel(_, x_hbm, g_hbm, rate_hbm, msg_ref, ain_ref, gt_ref, packed_ref, x_ref, g_ref, rate_ref, xt_ref, rate2_ref, rows_ref, blk_ref, sems):
    copies = [
        pltpu.make_async_copy(source, target, sems.at[i])
        for i, (source, target) in enumerate(((rate_hbm, rate_ref), (g_hbm, g_ref), (x_hbm, x_ref)))
    ]
    for copy in copies:
        copy.start()
    copies[0].wait()
    rate2_ref[...] = double(rate_ref[...])
    packed_ref[...] = pack(rate2_ref)
    copies[1].wait()
    gt_ref[...] = transposed(g_ref[...])
    copies[2].wait()
    xt_ref[...] = transposed(x_ref[...])
    full = (SUBLANES, LANES)
    low = low_half(full)
    block = lax.broadcasted_iota(jnp.int32, full, 0)
    after = (SUBLANES - 1 - block).astype(jnp.float32)
    after_all = jnp.where(low, after + SUBLANES, after)
    zero = jnp.zeros(full, jnp.float32)
    for first in range(0, POLES, 8):
        poles = range(first, first + 8)
        decay = [jnp.broadcast_to(jnp.exp(-rate2_ref[pl.ds(k, 1), :]), full) for k in poles]
        total = [zero] * 8
        slope = [zero] * 8
        value = [zero] * 8
        tilt = [zero] * 8
        for j in reversed(range(STEP)):
            g = gt_ref[pl.ds(j, SUBLANES, stride=STEP), :]
            x = xt_ref[pl.ds(j, SUBLANES, stride=STEP), :]
            for i in range(8):
                slope[i] = decay[i] * (slope[i] + total[i])
                total[i] = decay[i] * total[i] + g
                value[i] = value[i] + x * total[i]
                tilt[i] = tilt[i] + x * slope[i]
        for i, k in enumerate(poles):
            blk_ref[0, k] = total[i]
            blk_ref[1, k] = slope[i]
            blk_ref[2, k] = value[i]
            blk_ref[3, k] = tilt[i]
        state = [zero] * 8
        lean = [zero] * 8
        for j in range(STEP):
            x = xt_ref[pl.ds(j, SUBLANES, stride=STEP), :]
            for i in range(8):
                state[i] = decay[i] * (state[i] + x)
                lean[i] = decay[i] * lean[i] + state[i]
        for i, k in enumerate(poles):
            blk_ref[4, k] = state[i]
            blk_ref[5, k] = lean[i]
    for k in range(POLES):
        rate = rate2_ref[pl.ds(k, 1), :]
        total, slope = blk_ref[0, k], blk_ref[1, k]
        state, lean = blk_ref[4, k], blk_ref[5, k]
        for shift in (1, 2, 4):
            far = jnp.where(block < SUBLANES - shift, jnp.exp(-(STEP * shift) * rate), 0.0)
            moved = pltpu.roll(total, SUBLANES - shift, 0)
            turned = pltpu.roll(slope, SUBLANES - shift, 0)
            slope = slope + far * (turned + float(STEP * shift) * moved)
            total = total + far * moved
        rows_ref[0, pl.ds(k, 1), :] = total[0:1]
        rows_ref[1, pl.ds(k, 1), :] = slope[0:1]
        inside = block < SUBLANES - 1
        moved = jnp.where(inside, pltpu.roll(total, SUBLANES - 1, 0), 0.0)
        turned = jnp.where(inside, pltpu.roll(slope, SUBLANES - 1, 0), 0.0)
        late = jnp.where(low, pltpu.roll(jnp.broadcast_to(total[0:1], full), CHANNELS, 1), 0.0)
        late_slope = jnp.where(low, pltpu.roll(jnp.broadcast_to(slope[0:1], full), CHANNELS, 1), 0.0)
        reach = jnp.exp(-(float(STEP) * after) * rate)
        coming = moved + reach * late
        coming_slope = turned + reach * (late_slope + (float(STEP) * after) * late)
        ain_ref[k] = coming
        value = blk_ref[2, k] + state * coming
        tilt = blk_ref[3, k] + lean * coming + state * coming_slope
        away = float(STEP) * after_all
        weight = jnp.exp(-away * rate)
        rows_ref[2, pl.ds(k, 1), :] = jnp.sum(weight * state, axis=0, keepdims=True)
        rows_ref[3, pl.ds(k, 1), :] = jnp.sum(weight * (lean + away * state), axis=0, keepdims=True)
        rows_ref[4, pl.ds(k, 1), :] = jnp.sum(value, axis=0, keepdims=True)
        rows_ref[5, pl.ds(k, 1), :] = jnp.sum(tilt, axis=0, keepdims=True)
    rates = rate2_ref[...]
    low_rows = low_half(rates.shape)
    jump = jnp.where(low_rows, 1.0, jnp.exp(-float(HALF) * rates))
    length = jnp.where(low_rows, 0.0, float(HALF))
    rows_ref[1] = jump * (rows_ref[1] + length * rows_ref[0])
    rows_ref[0] = jump * rows_ref[0]
    for q in range(6):
        both = rows_ref[q] + pltpu.roll(rows_ref[q], CHANNELS, 1)
        rows_ref[q] = both
        packed = pack(rows_ref.at[q])
        for d in range(ROWS):
            msg_ref[d, pl.ds(q * SUBLANES, SUBLANES), :] = packed


def combine(recv_ref, rate, span):
    part = lambda d, q: recv_ref[d, pl.ds(q * SUBLANES, SUBLANES), :]
    decay = jnp.exp(-span * rate)
    coming = jnp.zeros_like(rate)
    coming_slope = jnp.zeros_like(rate)
    value = part(ROWS - 1, 4)
    tilt = part(ROWS - 1, 5)
    arriving = [coming] * ROWS
    for d in reversed(range(ROWS - 1)):
        coming_slope = part(d + 1, 1) + decay * (coming_slope + span * coming)
        coming = part(d + 1, 0) + decay * coming
        arriving[d] = coming
        value = value + part(d, 4) + part(d, 2) * coming
        tilt = tilt + part(d, 5) + part(d, 3) * coming + part(d, 2) * coming_slope
    slope = part(0, 1) + decay * (coming_slope + span * coming)
    total = part(0, 0) + decay * coming
    state = part(0, 2)
    lean = part(0, 3)
    for d in range(1, ROWS):
        lean = part(d, 3) + decay * (lean + span * state)
        state = part(d, 2) + decay * state
    return total, slope, state, lean, value, tilt, arriving


def pick(at, choices):
    out = choices[0]
    for d in range(1, ROWS):
        out = jnp.where(at == d, choices[d], out)
    return out


def row_kernel(at_ref, recv_ref, rate_ref, msg_ref, arrive_ref):
    rate = rate_ref[...]
    *sums, arriving = combine(recv_ref, rate, float(CHUNK))
    for q, packed in enumerate(sums):
        for d in range(ROWS):
            msg_ref[d, pl.ds(q * SUBLANES, SUBLANES), :] = packed
    arrive_ref[...] = pick(lax.rem(at_ref[0], ROWS), arriving)


def column_kernel(at_ref, recv_ref, rate_ref, arrive_ref, msg_ref, state_ref):
    rate = rate_ref[...]
    sums = combine(recv_ref, rate, float(CHUNK * ROWS))
    for q in range(2):
        for d in range(GROUP):
            msg_ref[d, pl.ds(q * SUBLANES, SUBLANES), :] = sums[4 + q]
    after = float(CHUNK) * (ROWS - 1 - lax.rem(at_ref[0], ROWS)).astype(jnp.float32)
    state_ref[...] = arrive_ref[...] + jnp.exp(-after * rate) * pick(lax.div(at_ref[0], ROWS), sums[6])


def post_kernel(gt_ref, rate_ref, weight_ref, ain_ref, state_ref, out_ref, yt_ref, rate2_ref, weight2_ref):
    rate2_ref[...] = double(rate_ref[...])
    weight2_ref[...] = double(weight_ref[...])
    full = (SUBLANES, LANES)
    low = low_half(full)
    low_row = low_half((1, LANES))
    after = (SUBLANES - 1 - lax.broadcasted_iota(jnp.int32, full, 0)).astype(jnp.float32)
    away = float(STEP) * jnp.where(low, after + SUBLANES, after)
    for first in range(0, POLES, 8):
        poles = range(first, first + 8)
        decay = [jnp.broadcast_to(jnp.exp(-rate2_ref[pl.ds(k, 1), :]), full) for k in poles]
        weight = [jnp.broadcast_to(weight2_ref[pl.ds(k, 1), :], full) for k in poles]
        total = []
        for k in poles:
            row = state_ref[pl.ds(k // 2, 1), :]
            other = pltpu.roll(row, CHANNELS, 1)
            both = jnp.where(low_row, row, other) if k % 2 == 0 else jnp.where(low_row, other, row)
            total.append(ain_ref[k] + jnp.exp(-away * rate2_ref[pl.ds(k, 1), :]) * both)
        for j in reversed(range(STEP)):
            at = pl.ds(j, SUBLANES, stride=STEP)
            g = gt_ref[at, :]
            for i in range(8):
                total[i] = decay[i] * total[i] + g
            terms = [weight[i] * total[i] for i in range(8)]
            while len(terms) > 1:
                terms = [terms[i] + terms[i + 1] for i in range(0, len(terms), 2)]
            yt_ref[at, :] = terms[0] if first == 0 else yt_ref[at, :] + terms[0]
    stacked = yt_ref[...].T
    out_ref[:, :HALF] = stacked[:CHANNELS].astype(jnp.bfloat16)
    out_ref[:, HALF:] = stacked[CHANNELS:].astype(jnp.bfloat16)


def final_kernel(recv_ref, one_ref, two_ref, three_ref, res_ref, log_ref):
    value = recv_ref[0, pl.ds(0, SUBLANES), :]
    tilt = recv_ref[0, pl.ds(SUBLANES, SUBLANES), :]
    for d in range(1, GROUP):
        value = value + recv_ref[d, pl.ds(0, SUBLANES), :]
        tilt = tilt + recv_ref[d, pl.ds(SUBLANES, SUBLANES), :]
    for k in range(POLES):
        lanes = slice(0, CHANNELS) if k % 2 == 0 else slice(CHANNELS, LANES)
        first = value[k // 2 : k // 2 + 1, lanes]
        second = tilt[k // 2 : k // 2 + 1, lanes]
        at = pl.ds(k, 1)
        res_ref[at, :] = one_ref[at, :] * first
        log_ref[at, :] = two_ref[at, :] * first - three_ref[at, :] * second


def vmem(count):
    return [pl.BlockSpec(memory_space=pltpu.VMEM)] * count


def f32(*shape):
    return jax.ShapeDtypeStruct(shape, jnp.float32)


def scratch(*shape):
    return pltpu.VMEM(shape, jnp.float32)


def body(inputs, grad_out, decay_rates, residues):
    rate = decay_rates.T
    residue = residues.T
    at = lax.axis_index("context").astype(jnp.int32).reshape(1)
    rows = [[y * ROWS + z for z in range(ROWS)] for y in range(ROWS)]
    columns = [[y * ROWS + z for y in range(ROWS)] for z in range(ROWS)]
    smem = [pl.BlockSpec(memory_space=pltpu.SMEM)]

    message, coming, turned, packed = pl.pallas_call(
        pre_kernel,
        out_shape=(f32(ROWS, 6 * SUBLANES, LANES), f32(POLES, SUBLANES, LANES), f32(HALF, LANES), f32(SUBLANES, LANES)),
        in_specs=smem + [pl.BlockSpec(memory_space=pltpu.HBM)] * 3,
        out_specs=tuple(vmem(4)),
        scratch_shapes=[
            pltpu.VMEM((CHANNELS, CHUNK), jnp.bfloat16),
            pltpu.VMEM((CHANNELS, CHUNK), jnp.bfloat16),
            scratch(POLES, CHANNELS),
            scratch(HALF, LANES),
            scratch(POLES, LANES),
            scratch(6, POLES, LANES),
            scratch(6, POLES, SUBLANES, LANES),
            pltpu.SemaphoreType.DMA((3,)),
        ],
        compiler_params=GRANT,
        name="pre",
    )(at, *(pltpu.with_memory_space_constraint(v, pltpu.HBM) for v in (inputs, grad_out, rate)))
    received = lax.all_to_all(message, "context", 0, 0, axis_index_groups=rows, tiled=True)
    message, arrived = pl.pallas_call(
        row_kernel,
        out_shape=(f32(ROWS, 6 * SUBLANES, LANES), f32(SUBLANES, LANES)),
        in_specs=smem + vmem(2),
        out_specs=tuple(vmem(2)),
        compiler_params=GRANT,
        name="row",
    )(at, received, packed)
    received = lax.all_to_all(message, "context", 0, 0, axis_index_groups=columns, tiled=True)
    message, state = pl.pallas_call(
        column_kernel,
        out_shape=(f32(GROUP, 2 * SUBLANES, LANES), f32(SUBLANES, LANES)),
        in_specs=smem + vmem(3),
        out_specs=tuple(vmem(2)),
        compiler_params=GRANT,
        name="column",
    )(at, received, packed, arrived)
    received = lax.all_to_all(message, "channel", 0, 0, tiled=True)

    gain = jnp.sqrt(-jnp.expm1(-2.0 * rate))
    decay = jnp.exp(-rate)
    grad_in = pl.pallas_call(
        post_kernel,
        out_shape=jax.ShapeDtypeStruct((CHANNELS, CHUNK), jnp.bfloat16),
        in_specs=vmem(5),
        out_specs=vmem(1)[0],
        scratch_shapes=[scratch(HALF, LANES), scratch(POLES, LANES), scratch(POLES, LANES)],
        compiler_params=GRANT,
        name="post",
    )(turned, rate, residue * gain, coming, state)
    norm = 1.0 / math.sqrt(CHUNK * ROWS * ROWS * GROUP)
    scaled = residue * rate * norm
    res_grad, log_grad = pl.pallas_call(
        final_kernel,
        out_shape=(f32(POLES, CHANNELS), f32(POLES, CHANNELS)),
        in_specs=vmem(4),
        out_specs=tuple(vmem(2)),
        compiler_params=GRANT,
        name="final",
    )(received, gain * norm, scaled * (decay * decay / gain), scaled * gain)
    return (grad_in, res_grad.T, log_grad.T)


def solution(mesh):
    return jax.shard_map(
        body,
        mesh=mesh,
        in_specs=(P("channel", "context"), P("channel", "context"), P(), P()),
        out_specs=(P("channel", "context"), P(), P()),
        check_vma=False,
    )
```

```python
import functools
import math

import jax
import jax.numpy as jnp
from jax import lax
from jax.experimental import pallas as pl
from jax.experimental.pallas import tpu as pltpu
from jax.sharding import PartitionSpec as P

LANES = 128
SUBLANES = 8
CHANNELS = 64
POLES = 16
STEP = 32
HALF = SUBLANES * STEP
CHUNK = 2 * HALF
BLOCKS = 4
BLOCK = HALF // BLOCKS
UNROLL = 4
ROWS = 8
GROUP = 8
GRANT = pltpu.CompilerParams(vmem_limit_bytes=8 << 20)


def low_half(shape):
    return lax.broadcasted_iota(jnp.int32, shape, len(shape) - 1) < CHANNELS


def double(rows):
    return jnp.concatenate([rows, rows], axis=1)


def pack(ref):
    even = ref[pl.ds(0, SUBLANES, stride=2), :]
    odd = ref[pl.ds(1, SUBLANES, stride=2), :]
    return jnp.where(low_half(even.shape), even, odd)


def transposed(block):
    stacked = jnp.concatenate([block[:, :HALF], block[:, HALF:]], axis=0)
    return stacked.astype(jnp.float32).T


def pre_kernel(_, x_hbm, g_hbm, rate_hbm, msg_ref, gt_ref, packed_ref, x_ref, g_ref, rate_ref, xt_ref, rows_ref, sems):
    copies = [
        pltpu.make_async_copy(source, target, sems.at[i])
        for i, (source, target) in enumerate(((rate_hbm, rate_ref), (g_hbm, g_ref), (x_hbm, x_ref)))
    ]
    for copy in copies:
        copy.start()
    copies[0].wait()
    rate = double(rate_ref[...])
    rows_ref[0] = rate
    packed_ref[...] = pack(rows_ref.at[0])
    decay = jnp.exp(-rate)
    copies[1].wait()
    gt_ref[...] = transposed(g_ref[...])
    copies[2].wait()
    xt_ref[...] = transposed(x_ref[...])

    def steps(outer, carry):
        total, slope, state, lean, value, tilt = (list(part) for part in carry)
        for inner in range(UNROLL):
            for b in range(BLOCKS):
                up = pl.ds(b * BLOCK + outer * UNROLL + inner, 1)
                down = pl.ds((b + 1) * BLOCK - 1 - outer * UNROLL - inner, 1)
                g, x, earlier = gt_ref[down, :], xt_ref[down, :], xt_ref[up, :]
                slope[b] = decay * (slope[b] + total[b])
                total[b] = decay * total[b] + g
                value[b % 2] = value[b % 2] + x * total[b]
                tilt[b % 2] = tilt[b % 2] + x * slope[b]
                state[b] = decay * (state[b] + earlier)
                lean[b] = decay * lean[b] + state[b]
        return total, slope, state, lean, value, tilt

    zero = jnp.zeros((POLES, LANES), jnp.float32)
    blank = [zero] * BLOCKS
    total, slope, state, lean, value, tilt = lax.fori_loop(
        0, BLOCK // UNROLL, steps, (blank, blank, blank, blank, [zero] * 2, [zero] * 2)
    )
    value = value[0] + value[1]
    tilt = tilt[0] + tilt[1]
    reach = jnp.exp(-float(BLOCK) * rate)
    coming, coming_slope = total[-1], slope[-1]
    behind, behind_lean = state[0], lean[0]
    for b in range(1, BLOCKS):
        back = BLOCKS - 1 - b
        value = value + state[back] * coming
        tilt = tilt + lean[back] * coming + state[back] * coming_slope
        coming_slope = slope[back] + reach * (coming_slope + float(BLOCK) * coming)
        coming = total[back] + reach * coming
        behind_lean = lean[b] + reach * (behind_lean + float(BLOCK) * behind)
        behind = state[b] + reach * behind
    low = low_half(zero.shape)
    turn = lambda v: pltpu.roll(v, CHANNELS, 1)
    late, late_slope = turn(coming), turn(coming_slope)
    value = value + jnp.where(low, behind * late, 0.0)
    tilt = tilt + jnp.where(low, behind_lean * late + behind * late_slope, 0.0)
    jump = jnp.exp(-float(HALF) * rate)
    sums = (
        coming + jump * late,
        coming_slope + jump * (late_slope + float(HALF) * late),
        jump * behind + turn(behind),
        jump * (behind_lean + float(HALF) * behind) + turn(behind_lean),
    )
    whole = [jnp.where(low, v, turn(v)) for v in sums] + [v + turn(v) for v in (value, tilt)]
    for q, v in enumerate(whole):
        rows_ref[q] = v
        packed = pack(rows_ref.at[q])
        for d in range(ROWS):
            msg_ref[d, pl.ds(q * SUBLANES, SUBLANES), :] = packed


def combine(recv_ref, rate, span):
    part = lambda d, q: recv_ref[d, pl.ds(q * SUBLANES, SUBLANES), :]
    decay = jnp.exp(-span * rate)
    coming = jnp.zeros_like(rate)
    coming_slope = jnp.zeros_like(rate)
    value = part(ROWS - 1, 4)
    tilt = part(ROWS - 1, 5)
    arriving = [coming] * ROWS
    for d in reversed(range(ROWS - 1)):
        coming_slope = part(d + 1, 1) + decay * (coming_slope + span * coming)
        coming = part(d + 1, 0) + decay * coming
        arriving[d] = coming
        value = value + part(d, 4) + part(d, 2) * coming
        tilt = tilt + part(d, 5) + part(d, 3) * coming + part(d, 2) * coming_slope
    slope = part(0, 1) + decay * (coming_slope + span * coming)
    total = part(0, 0) + decay * coming
    state = part(0, 2)
    lean = part(0, 3)
    for d in range(1, ROWS):
        lean = part(d, 3) + decay * (lean + span * state)
        state = part(d, 2) + decay * state
    return total, slope, state, lean, value, tilt, arriving


def pick(at, choices):
    out = choices[0]
    for d in range(1, ROWS):
        out = jnp.where(at == d, choices[d], out)
    return out


def row_kernel(at_ref, recv_ref, rate_ref, msg_ref, arrive_ref):
    rate = rate_ref[...]
    *sums, arriving = combine(recv_ref, rate, float(CHUNK))
    for q, packed in enumerate(sums):
        for d in range(ROWS):
            msg_ref[d, pl.ds(q * SUBLANES, SUBLANES), :] = packed
    arrive_ref[...] = pick(lax.rem(at_ref[0], ROWS), arriving)


def column_kernel(at_ref, recv_ref, rate_ref, arrive_ref, msg_ref, state_ref):
    rate = rate_ref[...]
    sums = combine(recv_ref, rate, float(CHUNK * ROWS))
    for q in range(2):
        for d in range(GROUP):
            msg_ref[d, pl.ds(q * SUBLANES, SUBLANES), :] = sums[4 + q]
    after = float(CHUNK) * (ROWS - 1 - lax.rem(at_ref[0], ROWS)).astype(jnp.float32)
    state_ref[...] = arrive_ref[...] + jnp.exp(-after * rate) * pick(lax.div(at_ref[0], ROWS), sums[6])


def post_kernel(gt_ref, rate_ref, weight_ref, state_ref, out_ref, yt_ref):
    full = (SUBLANES, LANES)
    low = low_half(full)
    low_row = low_half((1, LANES))
    block = lax.broadcasted_iota(jnp.int32, full, 0)
    after = float(STEP) * (SUBLANES - 1 - block).astype(jnp.float32)
    away = jnp.where(low, after + float(HALF), after)
    rates = double(rate_ref[...])
    weights = double(weight_ref[...])
    decays = jnp.exp(-rates)
    spans = jnp.exp(-float(STEP) * rates)
    wide = lambda rows, k: jnp.broadcast_to(rows[k : k + 1], full)
    for first in range(0, POLES, 8):
        poles = range(first, first + 8)
        decay = [wide(decays, k) for k in poles]

        def ends(at, total):
            g = gt_ref[pl.ds(STEP - 1 - at, SUBLANES, stride=STEP), :]
            return [decay[i] * total[i] + g for i in range(8)]

        blank = [jnp.zeros(full, jnp.float32)] * 8
        local = lax.fori_loop(0, STEP, ends, blank, unroll=4)
        entry = []
        for i, k in enumerate(poles):
            total = local[i]
            far = wide(spans, k)
            for shift in (1, 2, 4):
                moved = pltpu.roll(total, SUBLANES - shift, 0)
                total = total + jnp.where(block < SUBLANES - shift, far * moved, 0.0)
                far = far * far
            inside = jnp.where(block < SUBLANES - 1, pltpu.roll(total, SUBLANES - 1, 0), 0.0)
            late = jnp.where(low, pltpu.roll(jnp.broadcast_to(total[0:1], full), CHANNELS, 1), 0.0)
            row = state_ref[pl.ds(k // 2, 1), :]
            other = pltpu.roll(row, CHANNELS, 1)
            both = jnp.where(low_row, row, other) if k % 2 == 0 else jnp.where(low_row, other, row)
            rate = rates[k : k + 1]
            entry.append(inside + jnp.exp(-after * rate) * late + jnp.exp(-away * rate) * both)
        weight = [wide(weights, k) for k in poles]

        def outputs(at, total):
            rows = pl.ds(STEP - 1 - at, SUBLANES, stride=STEP)
            g = gt_ref[rows, :]
            total = [decay[i] * total[i] + g for i in range(8)]
            terms = [weight[i] * total[i] for i in range(8)]
            while len(terms) > 1:
                terms = [terms[i] + terms[i + 1] for i in range(0, len(terms), 2)]
            yt_ref[rows, :] = terms[0] if first == 0 else yt_ref[rows, :] + terms[0]
            return total

        lax.fori_loop(0, STEP, outputs, entry, unroll=4)
    stacked = yt_ref[...].T
    out_ref[:, :HALF] = stacked[:CHANNELS].astype(jnp.bfloat16)
    out_ref[:, HALF:] = stacked[CHANNELS:].astype(jnp.bfloat16)


def final_kernel(recv_ref, one_ref, two_ref, three_ref, res_ref, log_ref):
    value = recv_ref[0, pl.ds(0, SUBLANES), :]
    tilt = recv_ref[0, pl.ds(SUBLANES, SUBLANES), :]
    for d in range(1, GROUP):
        value = value + recv_ref[d, pl.ds(0, SUBLANES), :]
        tilt = tilt + recv_ref[d, pl.ds(SUBLANES, SUBLANES), :]
    for k in range(POLES):
        lanes = slice(0, CHANNELS) if k % 2 == 0 else slice(CHANNELS, LANES)
        first = value[k // 2 : k // 2 + 1, lanes]
        second = tilt[k // 2 : k // 2 + 1, lanes]
        at = pl.ds(k, 1)
        res_ref[at, :] = one_ref[at, :] * first
        log_ref[at, :] = two_ref[at, :] * first - three_ref[at, :] * second


def vmem(count):
    return [pl.BlockSpec(memory_space=pltpu.VMEM)] * count


def f32(*shape):
    return jax.ShapeDtypeStruct(shape, jnp.float32)


def scratch(*shape):
    return pltpu.VMEM(shape, jnp.float32)


def body(inputs, grad_out, decay_rates, residues):
    rate = decay_rates.T
    residue = residues.T
    at = lax.axis_index("context").astype(jnp.int32).reshape(1)
    rows = [[y * ROWS + z for z in range(ROWS)] for y in range(ROWS)]
    columns = [[y * ROWS + z for y in range(ROWS)] for z in range(ROWS)]
    smem = [pl.BlockSpec(memory_space=pltpu.SMEM)]

    message, turned, packed = pl.pallas_call(
        pre_kernel,
        out_shape=(f32(ROWS, 6 * SUBLANES, LANES), f32(HALF, LANES), f32(SUBLANES, LANES)),
        in_specs=smem + [pl.BlockSpec(memory_space=pltpu.HBM)] * 3,
        out_specs=tuple(vmem(3)),
        scratch_shapes=[
            pltpu.VMEM((CHANNELS, CHUNK), jnp.bfloat16),
            pltpu.VMEM((CHANNELS, CHUNK), jnp.bfloat16),
            scratch(POLES, CHANNELS),
            scratch(HALF, LANES),
            scratch(6, POLES, LANES),
            pltpu.SemaphoreType.DMA((3,)),
        ],
        compiler_params=GRANT,
        name="pre",
    )(at, *(pltpu.with_memory_space_constraint(v, pltpu.HBM) for v in (inputs, grad_out, rate)))
    received = lax.all_to_all(message, "context", 0, 0, axis_index_groups=rows, tiled=True)
    message, arrived = pl.pallas_call(
        row_kernel,
        out_shape=(f32(ROWS, 6 * SUBLANES, LANES), f32(SUBLANES, LANES)),
        in_specs=smem + vmem(2),
        out_specs=tuple(vmem(2)),
        compiler_params=GRANT,
        name="row",
    )(at, received, packed)
    received = lax.all_to_all(message, "context", 0, 0, axis_index_groups=columns, tiled=True)
    message, state = pl.pallas_call(
        column_kernel,
        out_shape=(f32(GROUP, 2 * SUBLANES, LANES), f32(SUBLANES, LANES)),
        in_specs=smem + vmem(3),
        out_specs=tuple(vmem(2)),
        compiler_params=GRANT,
        name="column",
    )(at, received, packed, arrived)
    received = lax.all_to_all(message, "channel", 0, 0, tiled=True)

    gain = jnp.sqrt(-jnp.expm1(-2.0 * rate))
    decay = jnp.exp(-rate)
    grad_in = pl.pallas_call(
        post_kernel,
        out_shape=jax.ShapeDtypeStruct((CHANNELS, CHUNK), jnp.bfloat16),
        in_specs=vmem(4),
        out_specs=vmem(1)[0],
        scratch_shapes=[scratch(HALF, LANES)],
        compiler_params=GRANT,
        name="post",
    )(turned, rate, residue * gain, state)
    norm = 1.0 / math.sqrt(CHUNK * ROWS * ROWS * GROUP)
    scaled = residue * rate * norm
    res_grad, log_grad = pl.pallas_call(
        final_kernel,
        out_shape=(f32(POLES, CHANNELS), f32(POLES, CHANNELS)),
        in_specs=vmem(4),
        out_specs=tuple(vmem(2)),
        compiler_params=GRANT,
        name="final",
    )(received, gain * norm, scaled * (decay * decay / gain), scaled * gain)
    return (grad_in, res_grad.T, log_grad.T)


def solution(mesh):
    return jax.shard_map(
        body,
        mesh=mesh,
        in_specs=(P("channel", "context"), P("channel", "context"), P(), P()),
        out_specs=(P("channel", "context"), P(), P()),
        check_vma=False,
    )
```

```python
import functools
import math

import jax
import jax.numpy as jnp
from jax import lax
from jax.experimental import pallas as pl
from jax.experimental.pallas import tpu as pltpu
from jax.sharding import PartitionSpec as P

LANES = 128
SUBLANES = 8
CHANNELS = 64
POLES = 16
STEP = 32
HALF = SUBLANES * STEP
CHUNK = 2 * HALF
BLOCKS = 4
BLOCK = HALF // BLOCKS
UNROLL = 16
ROWS = 8
GROUP = 8
ROW_ORDER = [7, 6, 5, 4, 3, 2, 1, 0]
COLUMN_ORDER = [4, 3, 2, 1, 0, 7, 6, 5]
CHANNEL_ORDER = [5, 4, 3, 2, 1, 0, 7, 6]
GRANT = pltpu.CompilerParams(vmem_limit_bytes=8 << 20)


def low_half(shape):
    return lax.broadcasted_iota(jnp.int32, shape, len(shape) - 1) < CHANNELS


def double(rows):
    return jnp.concatenate([rows, rows], axis=1)


def pack(ref):
    even = ref[pl.ds(0, SUBLANES, stride=2), :]
    odd = ref[pl.ds(1, SUBLANES, stride=2), :]
    return jnp.where(low_half(even.shape), even, odd)


def transposed(block):
    stacked = jnp.concatenate([block[:, :HALF], block[:, HALF:]], axis=0)
    return stacked.astype(jnp.float32).T


def pre_kernel(_, x_hbm, g_hbm, rate_hbm, msg_ref, gt_ref, packed_ref, x_ref, g_ref, rate_ref, xt_ref, rows_ref, sems):
    copies = [
        pltpu.make_async_copy(source, target, sems.at[i])
        for i, (source, target) in enumerate(((rate_hbm, rate_ref), (g_hbm, g_ref), (x_hbm, x_ref)))
    ]
    for copy in copies:
        copy.start()
    copies[0].wait()
    rate = double(rate_ref[...])
    rows_ref[0] = rate
    packed_ref[...] = pack(rows_ref.at[0])
    decay = jnp.exp(-rate)
    copies[1].wait()
    gt_ref[...] = transposed(g_ref[...])
    copies[2].wait()
    xt_ref[...] = transposed(x_ref[...])

    def steps(outer, carry):
        total, slope, state, lean, value, tilt = (list(part) for part in carry)
        for inner in range(UNROLL):
            for b in range(BLOCKS):
                up = pl.ds(b * BLOCK + outer * UNROLL + inner, 1)
                down = pl.ds((b + 1) * BLOCK - 1 - outer * UNROLL - inner, 1)
                g, x, earlier = gt_ref[down, :], xt_ref[down, :], xt_ref[up, :]
                slope[b] = decay * (slope[b] + total[b])
                total[b] = decay * total[b] + g
                value[b % 2] = value[b % 2] + x * total[b]
                tilt[b % 2] = tilt[b % 2] + x * slope[b]
                state[b] = decay * (state[b] + earlier)
                lean[b] = decay * lean[b] + state[b]
        return total, slope, state, lean, value, tilt

    zero = jnp.zeros((POLES, LANES), jnp.float32)
    blank = [zero] * BLOCKS
    total, slope, state, lean, value, tilt = lax.fori_loop(
        0, BLOCK // UNROLL, steps, (blank, blank, blank, blank, [zero] * 2, [zero] * 2)
    )
    value = value[0] + value[1]
    tilt = tilt[0] + tilt[1]
    reach = jnp.exp(-float(BLOCK) * rate)
    coming, coming_slope = total[-1], slope[-1]
    behind, behind_lean = state[0], lean[0]
    for b in range(1, BLOCKS):
        back = BLOCKS - 1 - b
        value = value + state[back] * coming
        tilt = tilt + lean[back] * coming + state[back] * coming_slope
        coming_slope = slope[back] + reach * (coming_slope + float(BLOCK) * coming)
        coming = total[back] + reach * coming
        behind_lean = lean[b] + reach * (behind_lean + float(BLOCK) * behind)
        behind = state[b] + reach * behind
    low = low_half(zero.shape)
    turn = lambda v: pltpu.roll(v, CHANNELS, 1)
    late, late_slope = turn(coming), turn(coming_slope)
    value = value + jnp.where(low, behind * late, 0.0)
    tilt = tilt + jnp.where(low, behind_lean * late + behind * late_slope, 0.0)
    jump = jnp.exp(-float(HALF) * rate)
    sums = (
        coming + jump * late,
        coming_slope + jump * (late_slope + float(HALF) * late),
        jump * behind + turn(behind),
        jump * (behind_lean + float(HALF) * behind) + turn(behind_lean),
    )
    whole = [jnp.where(low, v, turn(v)) for v in sums] + [v + turn(v) for v in (value, tilt)]
    for q, v in enumerate(whole):
        rows_ref[q] = v
        packed = pack(rows_ref.at[q])
        for d in range(ROWS):
            msg_ref[d, pl.ds(q * SUBLANES, SUBLANES), :] = packed


def combine(recv_ref, rate, span, order):
    part = lambda d, q: recv_ref[order.index(d), pl.ds(q * SUBLANES, SUBLANES), :]
    decay = jnp.exp(-span * rate)
    coming = jnp.zeros_like(rate)
    coming_slope = jnp.zeros_like(rate)
    value = part(ROWS - 1, 4)
    tilt = part(ROWS - 1, 5)
    arriving = [coming] * ROWS
    for d in reversed(range(ROWS - 1)):
        coming_slope = part(d + 1, 1) + decay * (coming_slope + span * coming)
        coming = part(d + 1, 0) + decay * coming
        arriving[d] = coming
        value = value + part(d, 4) + part(d, 2) * coming
        tilt = tilt + part(d, 5) + part(d, 3) * coming + part(d, 2) * coming_slope
    slope = part(0, 1) + decay * (coming_slope + span * coming)
    total = part(0, 0) + decay * coming
    state = part(0, 2)
    lean = part(0, 3)
    for d in range(1, ROWS):
        lean = part(d, 3) + decay * (lean + span * state)
        state = part(d, 2) + decay * state
    return total, slope, state, lean, value, tilt, arriving


def pick(at, choices):
    out = choices[0]
    for d in range(1, ROWS):
        out = jnp.where(at == d, choices[d], out)
    return out


def row_kernel(at_ref, recv_ref, rate_ref, msg_ref, arrive_ref):
    rate = rate_ref[...]
    *sums, arriving = combine(recv_ref, rate, float(CHUNK), ROW_ORDER)
    for q, packed in enumerate(sums):
        for d in range(ROWS):
            msg_ref[d, pl.ds(q * SUBLANES, SUBLANES), :] = packed
    arrive_ref[...] = pick(lax.rem(at_ref[0], ROWS), arriving)


def column_kernel(at_ref, recv_ref, rate_ref, arrive_ref, msg_ref, state_ref):
    rate = rate_ref[...]
    sums = combine(recv_ref, rate, float(CHUNK * ROWS), COLUMN_ORDER)
    for q in range(2):
        for d in range(GROUP):
            msg_ref[d, pl.ds(q * SUBLANES, SUBLANES), :] = sums[4 + q]
    after = float(CHUNK) * (ROWS - 1 - lax.rem(at_ref[0], ROWS)).astype(jnp.float32)
    state_ref[...] = arrive_ref[...] + jnp.exp(-after * rate) * pick(lax.div(at_ref[0], ROWS), sums[6])


def post_kernel(gt_ref, rate_ref, weight_ref, state_ref, out_ref, yt_ref):
    full = (SUBLANES, LANES)
    low = low_half(full)
    low_row = low_half((1, LANES))
    block = lax.broadcasted_iota(jnp.int32, full, 0)
    after = float(STEP) * (SUBLANES - 1 - block).astype(jnp.float32)
    away = jnp.where(low, after + float(HALF), after)
    rates = double(rate_ref[...])
    weights = double(weight_ref[...])
    decays = jnp.exp(-rates)
    spans = jnp.exp(-float(STEP) * rates)
    wide = lambda rows, k: jnp.broadcast_to(rows[k : k + 1], full)
    for first in range(0, POLES, 8):
        poles = range(first, first + 8)
        decay = [wide(decays, k) for k in poles]

        def ends(at, total):
            g = gt_ref[pl.ds(STEP - 1 - at, SUBLANES, stride=STEP), :]
            return [decay[i] * total[i] + g for i in range(8)]

        blank = [jnp.zeros(full, jnp.float32)] * 8
        local = lax.fori_loop(0, STEP, ends, blank, unroll=4)
        entry = []
        for i, k in enumerate(poles):
            total = local[i]
            far = wide(spans, k)
            for shift in (1, 2, 4):
                moved = pltpu.roll(total, SUBLANES - shift, 0)
                total = total + jnp.where(block < SUBLANES - shift, far * moved, 0.0)
                far = far * far
            inside = jnp.where(block < SUBLANES - 1, pltpu.roll(total, SUBLANES - 1, 0), 0.0)
            late = jnp.where(low, pltpu.roll(jnp.broadcast_to(total[0:1], full), CHANNELS, 1), 0.0)
            row = state_ref[pl.ds(k // 2, 1), :]
            other = pltpu.roll(row, CHANNELS, 1)
            both = jnp.where(low_row, row, other) if k % 2 == 0 else jnp.where(low_row, other, row)
            rate = rates[k : k + 1]
            entry.append(inside + jnp.exp(-after * rate) * late + jnp.exp(-away * rate) * both)
        weight = [wide(weights, k) for k in poles]

        def outputs(at, total):
            rows = pl.ds(STEP - 1 - at, SUBLANES, stride=STEP)
            g = gt_ref[rows, :]
            total = [decay[i] * total[i] + g for i in range(8)]
            terms = [weight[i] * total[i] for i in range(8)]
            while len(terms) > 1:
                terms = [terms[i] + terms[i + 1] for i in range(0, len(terms), 2)]
            yt_ref[rows, :] = terms[0] if first == 0 else yt_ref[rows, :] + terms[0]
            return total

        lax.fori_loop(0, STEP, outputs, entry, unroll=4)
    stacked = yt_ref[...].T
    out_ref[:, :HALF] = stacked[:CHANNELS].astype(jnp.bfloat16)
    out_ref[:, HALF:] = stacked[CHANNELS:].astype(jnp.bfloat16)


def final_kernel(recv_ref, one_ref, two_ref, three_ref, res_ref, log_ref):
    value = recv_ref[0, pl.ds(0, SUBLANES), :]
    tilt = recv_ref[0, pl.ds(SUBLANES, SUBLANES), :]
    for d in range(1, GROUP):
        value = value + recv_ref[d, pl.ds(0, SUBLANES), :]
        tilt = tilt + recv_ref[d, pl.ds(SUBLANES, SUBLANES), :]
    for k in range(POLES):
        lanes = slice(0, CHANNELS) if k % 2 == 0 else slice(CHANNELS, LANES)
        first = value[k // 2 : k // 2 + 1, lanes]
        second = tilt[k // 2 : k // 2 + 1, lanes]
        at = pl.ds(k, 1)
        res_ref[at, :] = one_ref[at, :] * first
        log_ref[at, :] = two_ref[at, :] * first - three_ref[at, :] * second


def vmem(count):
    return [pl.BlockSpec(memory_space=pltpu.VMEM)] * count


def f32(*shape):
    return jax.ShapeDtypeStruct(shape, jnp.float32)


def scratch(*shape):
    return pltpu.VMEM(shape, jnp.float32)


def first_call(at, x, g, rate, name="pre"):
    return pl.pallas_call(
        pre_kernel,
        out_shape=(f32(ROWS, 6 * SUBLANES, LANES), f32(HALF, LANES), f32(SUBLANES, LANES)),
        in_specs=[pl.BlockSpec(memory_space=pltpu.SMEM)] + [pl.BlockSpec(memory_space=pltpu.HBM)] * 3,
        out_specs=tuple(vmem(3)),
        scratch_shapes=[
            pltpu.VMEM((CHANNELS, CHUNK), jnp.bfloat16),
            pltpu.VMEM((CHANNELS, CHUNK), jnp.bfloat16),
            scratch(POLES, CHANNELS),
            scratch(HALF, LANES),
            scratch(6, POLES, LANES),
            pltpu.SemaphoreType.DMA((3,)),
        ],
        compiler_params=GRANT,
        name=name,
    )(at, x, g, rate)


def body(inputs, grad_out, decay_rates, residues):
    rate = decay_rates.T
    residue = residues.T
    at = lax.axis_index("context").astype(jnp.int32).reshape(1)
    rows = [[y * ROWS + z for z in ROW_ORDER] for y in range(ROWS)]
    columns = [[y * ROWS + z for y in COLUMN_ORDER] for z in range(ROWS)]
    smem = [pl.BlockSpec(memory_space=pltpu.SMEM)]

    message, turned, packed = first_call(
        at, *(pltpu.with_memory_space_constraint(v, pltpu.HBM) for v in (inputs, grad_out, rate))
    )
    received = lax.all_to_all(message, "context", 0, 0, axis_index_groups=rows, tiled=True)
    message, arrived = pl.pallas_call(
        row_kernel,
        out_shape=(f32(ROWS, 6 * SUBLANES, LANES), f32(SUBLANES, LANES)),
        in_specs=smem + vmem(2),
        out_specs=tuple(vmem(2)),
        compiler_params=GRANT,
        name="row",
    )(at, received, packed)
    received = lax.all_to_all(message, "context", 0, 0, axis_index_groups=columns, tiled=True)
    message, state = pl.pallas_call(
        column_kernel,
        out_shape=(f32(GROUP, 2 * SUBLANES, LANES), f32(SUBLANES, LANES)),
        in_specs=smem + vmem(3),
        out_specs=tuple(vmem(2)),
        compiler_params=GRANT,
        name="column",
    )(at, received, packed, arrived)
    received = lax.all_to_all(message, "channel", 0, 0, axis_index_groups=[CHANNEL_ORDER], tiled=True)

    gain = jnp.sqrt(-jnp.expm1(-2.0 * rate))
    decay = jnp.exp(-rate)
    grad_in = pl.pallas_call(
        post_kernel,
        out_shape=jax.ShapeDtypeStruct((CHANNELS, CHUNK), jnp.bfloat16),
        in_specs=vmem(4),
        out_specs=vmem(1)[0],
        scratch_shapes=[scratch(HALF, LANES)],
        compiler_params=GRANT,
        name="post",
    )(turned, rate, residue * gain, state)
    norm = 1.0 / math.sqrt(CHUNK * ROWS * ROWS * GROUP)
    scaled = residue * rate * norm
    res_grad, log_grad = pl.pallas_call(
        final_kernel,
        out_shape=(f32(POLES, CHANNELS), f32(POLES, CHANNELS)),
        in_specs=vmem(4),
        out_specs=tuple(vmem(2)),
        compiler_params=GRANT,
        name="final",
    )(received, gain * norm, scaled * (decay * decay / gain), scaled * gain)
    return (grad_in, res_grad.T, log_grad.T)


def solution(mesh):
    return jax.shard_map(
        body,
        mesh=mesh,
        in_specs=(P("channel", "context"), P("channel", "context"), P(), P()),
        out_specs=(P("channel", "context"), P(), P()),
        check_vma=False,
    )
```

```python
import functools
import math

import jax
import jax.numpy as jnp
from jax import lax
from jax.experimental import pallas as pl
from jax.experimental.pallas import tpu as pltpu
from jax.sharding import PartitionSpec as P

LANES = 128
SUBLANES = 8
CHANNELS = 64
POLES = 16
STEP = 32
HALF = SUBLANES * STEP
CHUNK = 2 * HALF
BLOCKS = 4
BLOCK = HALF // BLOCKS
UNROLL = 16
POSTU = 8
ROWS = 8
GROUP = 8
ROW_ORDER = [6, 5, 4, 3, 2, 1, 0, 7]
COLUMN_ORDER = [4, 3, 2, 1, 0, 7, 6, 5]
CHANNEL_ORDER = [5, 4, 3, 2, 1, 0, 7, 6]
GRANT = pltpu.CompilerParams(vmem_limit_bytes=8 << 20)


def low_half(shape):
    return lax.broadcasted_iota(jnp.int32, shape, len(shape) - 1) < CHANNELS


def double(rows):
    return jnp.concatenate([rows, rows], axis=1)


def pack(ref):
    even = ref[pl.ds(0, SUBLANES, stride=2), :]
    odd = ref[pl.ds(1, SUBLANES, stride=2), :]
    return jnp.where(low_half(even.shape), even, odd)


def transposed(block):
    stacked = jnp.concatenate([block[:, :HALF], block[:, HALF:]], axis=0)
    return stacked.astype(jnp.float32).T


def pre_kernel(_, x_hbm, g_hbm, rate_hbm, msg_ref, gt_ref, packed_ref, x_ref, g_ref, rate_ref, xt_ref, rows_ref, sems):
    copies = [
        pltpu.make_async_copy(source, target, sems.at[i])
        for i, (source, target) in enumerate(((rate_hbm, rate_ref), (g_hbm, g_ref), (x_hbm, x_ref)))
    ]
    for copy in copies:
        copy.start()
    copies[0].wait()
    rate = double(rate_ref[...])
    rows_ref[0] = rate
    packed_ref[...] = pack(rows_ref.at[0])
    decay = jnp.exp(-rate)
    copies[1].wait()
    gt_ref[...] = transposed(g_ref[...])
    copies[2].wait()
    xt_ref[...] = transposed(x_ref[...])

    def steps(outer, carry):
        total, slope, state, lean, value, tilt = (list(part) for part in carry)
        for inner in range(UNROLL):
            for b in range(BLOCKS):
                up = pl.ds(b * BLOCK + outer * UNROLL + inner, 1)
                down = pl.ds((b + 1) * BLOCK - 1 - outer * UNROLL - inner, 1)
                g, x, earlier = gt_ref[down, :], xt_ref[down, :], xt_ref[up, :]
                slope[b] = decay * (slope[b] + total[b])
                total[b] = decay * total[b] + g
                value[b % 2] = value[b % 2] + x * total[b]
                tilt[b % 2] = tilt[b % 2] + x * slope[b]
                state[b] = decay * (state[b] + earlier)
                lean[b] = decay * lean[b] + state[b]
        return total, slope, state, lean, value, tilt

    zero = jnp.zeros((POLES, LANES), jnp.float32)
    blank = [zero] * BLOCKS
    total, slope, state, lean, value, tilt = lax.fori_loop(
        0, BLOCK // UNROLL, steps, (blank, blank, blank, blank, [zero] * 2, [zero] * 2)
    )
    value = value[0] + value[1]
    tilt = tilt[0] + tilt[1]
    reach = jnp.exp(-float(BLOCK) * rate)
    coming, coming_slope = total[-1], slope[-1]
    behind, behind_lean = state[0], lean[0]
    for b in range(1, BLOCKS):
        back = BLOCKS - 1 - b
        value = value + state[back] * coming
        tilt = tilt + lean[back] * coming + state[back] * coming_slope
        coming_slope = slope[back] + reach * (coming_slope + float(BLOCK) * coming)
        coming = total[back] + reach * coming
        behind_lean = lean[b] + reach * (behind_lean + float(BLOCK) * behind)
        behind = state[b] + reach * behind
    low = low_half(zero.shape)
    turn = lambda v: pltpu.roll(v, CHANNELS, 1)
    late, late_slope = turn(coming), turn(coming_slope)
    value = value + jnp.where(low, behind * late, 0.0)
    tilt = tilt + jnp.where(low, behind_lean * late + behind * late_slope, 0.0)
    jump = jnp.exp(-float(HALF) * rate)
    sums = (
        coming + jump * late,
        coming_slope + jump * (late_slope + float(HALF) * late),
        jump * behind + turn(behind),
        jump * (behind_lean + float(HALF) * behind) + turn(behind_lean),
    )
    whole = [jnp.where(low, v, turn(v)) for v in sums] + [v + turn(v) for v in (value, tilt)]
    for q, v in enumerate(whole):
        rows_ref[q] = v
        packed = pack(rows_ref.at[q])
        for d in range(ROWS):
            msg_ref[d, pl.ds(q * SUBLANES, SUBLANES), :] = packed


def combine(recv_ref, rate, span, order):
    part = lambda d, q: recv_ref[order.index(d), pl.ds(q * SUBLANES, SUBLANES), :]
    decay = jnp.exp(-span * rate)
    coming = jnp.zeros_like(rate)
    coming_slope = jnp.zeros_like(rate)
    value = part(ROWS - 1, 4)
    tilt = part(ROWS - 1, 5)
    arriving = [coming] * ROWS
    for d in reversed(range(ROWS - 1)):
        coming_slope = part(d + 1, 1) + decay * (coming_slope + span * coming)
        coming = part(d + 1, 0) + decay * coming
        arriving[d] = coming
        value = value + part(d, 4) + part(d, 2) * coming
        tilt = tilt + part(d, 5) + part(d, 3) * coming + part(d, 2) * coming_slope
    slope = part(0, 1) + decay * (coming_slope + span * coming)
    total = part(0, 0) + decay * coming
    state = part(0, 2)
    lean = part(0, 3)
    for d in range(1, ROWS):
        lean = part(d, 3) + decay * (lean + span * state)
        state = part(d, 2) + decay * state
    return total, slope, state, lean, value, tilt, arriving


def pick(at, choices):
    out = choices[0]
    for d in range(1, ROWS):
        out = jnp.where(at == d, choices[d], out)
    return out


def row_kernel(at_ref, recv_ref, rate_ref, msg_ref, arrive_ref):
    rate = rate_ref[...]
    *sums, arriving = combine(recv_ref, rate, float(CHUNK), ROW_ORDER)
    for q, packed in enumerate(sums):
        for d in range(ROWS):
            msg_ref[d, pl.ds(q * SUBLANES, SUBLANES), :] = packed
    arrive_ref[...] = pick(lax.rem(at_ref[0], ROWS), arriving)


def column_kernel(at_ref, recv_ref, rate_ref, arrive_ref, msg_ref, state_ref):
    rate = rate_ref[...]
    sums = combine(recv_ref, rate, float(CHUNK * ROWS), COLUMN_ORDER)
    for q in range(2):
        for d in range(GROUP):
            msg_ref[d, pl.ds(q * SUBLANES, SUBLANES), :] = sums[4 + q]
    after = float(CHUNK) * (ROWS - 1 - lax.rem(at_ref[0], ROWS)).astype(jnp.float32)
    state_ref[...] = arrive_ref[...] + jnp.exp(-after * rate) * pick(lax.div(at_ref[0], ROWS), sums[6])


def post_kernel(gt_ref, rate_ref, weight_ref, state_ref, out_ref, yt_ref):
    full = (SUBLANES, LANES)
    low = low_half(full)
    low_row = low_half((1, LANES))
    block = lax.broadcasted_iota(jnp.int32, full, 0)
    after = float(STEP) * (SUBLANES - 1 - block).astype(jnp.float32)
    away = jnp.where(low, after + float(HALF), after)
    rates = double(rate_ref[...])
    weights = double(weight_ref[...])
    decays = jnp.exp(-rates)
    spans = jnp.exp(-float(STEP) * rates)
    wide = lambda rows, k: jnp.broadcast_to(rows[k : k + 1], full)
    for first in range(0, POLES, 8):
        poles = range(first, first + 8)
        decay = [wide(decays, k) for k in poles]

        def ends(at, total):
            g = gt_ref[pl.ds(STEP - 1 - at, SUBLANES, stride=STEP), :]
            return [decay[i] * total[i] + g for i in range(8)]

        blank = [jnp.zeros(full, jnp.float32)] * 8
        local = lax.fori_loop(0, STEP, ends, blank, unroll=POSTU)
        entry = []
        for i, k in enumerate(poles):
            total = local[i]
            far = wide(spans, k)
            for shift in (1, 2, 4):
                moved = pltpu.roll(total, SUBLANES - shift, 0)
                total = total + jnp.where(block < SUBLANES - shift, far * moved, 0.0)
                far = far * far
            inside = jnp.where(block < SUBLANES - 1, pltpu.roll(total, SUBLANES - 1, 0), 0.0)
            late = jnp.where(low, pltpu.roll(jnp.broadcast_to(total[0:1], full), CHANNELS, 1), 0.0)
            row = state_ref[pl.ds(k // 2, 1), :]
            other = pltpu.roll(row, CHANNELS, 1)
            both = jnp.where(low_row, row, other) if k % 2 == 0 else jnp.where(low_row, other, row)
            rate = rates[k : k + 1]
            entry.append(inside + jnp.exp(-after * rate) * late + jnp.exp(-away * rate) * both)
        weight = [wide(weights, k) for k in poles]

        def outputs(at, total):
            rows = pl.ds(STEP - 1 - at, SUBLANES, stride=STEP)
            g = gt_ref[rows, :]
            total = [decay[i] * total[i] + g for i in range(8)]
            terms = [weight[i] * total[i] for i in range(8)]
            while len(terms) > 1:
                terms = [terms[i] + terms[i + 1] for i in range(0, len(terms), 2)]
            yt_ref[rows, :] = terms[0] if first == 0 else yt_ref[rows, :] + terms[0]
            return total

        lax.fori_loop(0, STEP, outputs, entry, unroll=POSTU)
    stacked = yt_ref[...].T
    out_ref[:, :HALF] = stacked[:CHANNELS].astype(jnp.bfloat16)
    out_ref[:, HALF:] = stacked[CHANNELS:].astype(jnp.bfloat16)


def final_kernel(recv_ref, one_ref, two_ref, three_ref, res_ref, log_ref):
    value = recv_ref[0, pl.ds(0, SUBLANES), :]
    tilt = recv_ref[0, pl.ds(SUBLANES, SUBLANES), :]
    for d in range(1, GROUP):
        value = value + recv_ref[d, pl.ds(0, SUBLANES), :]
        tilt = tilt + recv_ref[d, pl.ds(SUBLANES, SUBLANES), :]
    for k in range(POLES):
        lanes = slice(0, CHANNELS) if k % 2 == 0 else slice(CHANNELS, LANES)
        first = value[k // 2 : k // 2 + 1, lanes]
        second = tilt[k // 2 : k // 2 + 1, lanes]
        at = pl.ds(k, 1)
        res_ref[at, :] = one_ref[at, :] * first
        log_ref[at, :] = two_ref[at, :] * first - three_ref[at, :] * second


def vmem(count):
    return [pl.BlockSpec(memory_space=pltpu.VMEM)] * count


def f32(*shape):
    return jax.ShapeDtypeStruct(shape, jnp.float32)


def scratch(*shape):
    return pltpu.VMEM(shape, jnp.float32)


def first_call(at, x, g, rate, name="pre"):
    return pl.pallas_call(
        pre_kernel,
        out_shape=(f32(ROWS, 6 * SUBLANES, LANES), f32(HALF, LANES), f32(SUBLANES, LANES)),
        in_specs=[pl.BlockSpec(memory_space=pltpu.SMEM)] + [pl.BlockSpec(memory_space=pltpu.HBM)] * 3,
        out_specs=tuple(vmem(3)),
        scratch_shapes=[
            pltpu.VMEM((CHANNELS, CHUNK), jnp.bfloat16),
            pltpu.VMEM((CHANNELS, CHUNK), jnp.bfloat16),
            scratch(POLES, CHANNELS),
            scratch(HALF, LANES),
            scratch(6, POLES, LANES),
            pltpu.SemaphoreType.DMA((3,)),
        ],
        compiler_params=GRANT,
        name=name,
    )(at, x, g, rate)


def body(inputs, grad_out, decay_rates, residues):
    rate = decay_rates.T
    residue = residues.T
    at = lax.axis_index("context").astype(jnp.int32).reshape(1)
    rows = [[y * ROWS + z for z in ROW_ORDER] for y in range(ROWS)]
    columns = [[y * ROWS + z for y in COLUMN_ORDER] for z in range(ROWS)]
    smem = [pl.BlockSpec(memory_space=pltpu.SMEM)]

    message, turned, packed = first_call(
        at, *(pltpu.with_memory_space_constraint(v, pltpu.HBM) for v in (inputs, grad_out, rate))
    )
    received = lax.all_to_all(message, "context", 0, 0, axis_index_groups=rows, tiled=True)
    message, arrived = pl.pallas_call(
        row_kernel,
        out_shape=(f32(ROWS, 6 * SUBLANES, LANES), f32(SUBLANES, LANES)),
        in_specs=smem + vmem(2),
        out_specs=tuple(vmem(2)),
        compiler_params=GRANT,
        name="row",
    )(at, received, packed)
    received = lax.all_to_all(message, "context", 0, 0, axis_index_groups=columns, tiled=True)
    message, state = pl.pallas_call(
        column_kernel,
        out_shape=(f32(GROUP, 2 * SUBLANES, LANES), f32(SUBLANES, LANES)),
        in_specs=smem + vmem(3),
        out_specs=tuple(vmem(2)),
        compiler_params=GRANT,
        name="column",
    )(at, received, packed, arrived)
    received = lax.all_to_all(message, "channel", 0, 0, axis_index_groups=[CHANNEL_ORDER], tiled=True)

    gain = jnp.sqrt(-jnp.expm1(-2.0 * rate))
    decay = jnp.exp(-rate)
    grad_in = pl.pallas_call(
        post_kernel,
        out_shape=jax.ShapeDtypeStruct((CHANNELS, CHUNK), jnp.bfloat16),
        in_specs=vmem(4),
        out_specs=vmem(1)[0],
        scratch_shapes=[scratch(HALF, LANES)],
        compiler_params=GRANT,
        name="post",
    )(turned, rate, residue * gain, state)
    norm = 1.0 / math.sqrt(CHUNK * ROWS * ROWS * GROUP)
    scaled = residue * rate * norm
    res_grad, log_grad = pl.pallas_call(
        final_kernel,
        out_shape=(f32(POLES, CHANNELS), f32(POLES, CHANNELS)),
        in_specs=vmem(4),
        out_specs=tuple(vmem(2)),
        compiler_params=GRANT,
        name="final",
    )(received, gain * norm, scaled * (decay * decay / gain), scaled * gain)
    return (grad_in, res_grad.T, log_grad.T)


def solution(mesh):
    return jax.shard_map(
        body,
        mesh=mesh,
        in_specs=(P("channel", "context"), P("channel", "context"), P(), P()),
        out_specs=(P("channel", "context"), P(), P()),
        check_vma=False,
    )
```

```python
import functools
import math

import jax
import jax.numpy as jnp
from jax import lax
from jax.experimental import pallas as pl
from jax.experimental.pallas import tpu as pltpu
from jax.sharding import PartitionSpec as P

LANES = 128
SUBLANES = 8
CHANNELS = 64
POLES = 16
STEP = 32
HALF = SUBLANES * STEP
CHUNK = 2 * HALF
BLOCKS = 4
BLOCK = HALF // BLOCKS
UNROLL = 16
POSTU = 8
ROWS = 8
GROUP = 8
ROW_ORDER = [6, 5, 4, 3, 2, 1, 0, 7]
COLUMN_ORDER = [4, 5, 3, 2, 0, 1, 7, 6]
CHANNEL_ORDER = [5, 7, 1, 3, 4, 6, 0, 2]
GRANT = pltpu.CompilerParams(vmem_limit_bytes=8 << 20)


def low_half(shape):
    return lax.broadcasted_iota(jnp.int32, shape, len(shape) - 1) < CHANNELS


def double(rows):
    return jnp.concatenate([rows, rows], axis=1)


def pack(ref):
    even = ref[pl.ds(0, SUBLANES, stride=2), :]
    odd = ref[pl.ds(1, SUBLANES, stride=2), :]
    return jnp.where(low_half(even.shape), even, odd)


def transposed(block):
    stacked = jnp.concatenate([block[:, :HALF], block[:, HALF:]], axis=0)
    return stacked.astype(jnp.float32).T


def pre_kernel(_, x_hbm, g_hbm, rate_hbm, msg_ref, gt_ref, packed_ref, x_ref, g_ref, rate_ref, xt_ref, rows_ref, sems):
    copies = [
        pltpu.make_async_copy(source, target, sems.at[i])
        for i, (source, target) in enumerate(((rate_hbm, rate_ref), (g_hbm, g_ref), (x_hbm, x_ref)))
    ]
    for copy in copies:
        copy.start()
    copies[0].wait()
    rate = double(rate_ref[...])
    rows_ref[0] = rate
    packed_ref[...] = pack(rows_ref.at[0])
    decay = jnp.exp(-rate)
    copies[1].wait()
    gt_ref[...] = transposed(g_ref[...])
    copies[2].wait()
    xt_ref[...] = transposed(x_ref[...])

    def steps(outer, carry):
        total, slope, state, lean, value, tilt = (list(part) for part in carry)
        for inner in range(UNROLL):
            for b in range(BLOCKS):
                up = pl.ds(b * BLOCK + outer * UNROLL + inner, 1)
                down = pl.ds((b + 1) * BLOCK - 1 - outer * UNROLL - inner, 1)
                g, x, earlier = gt_ref[down, :], xt_ref[down, :], xt_ref[up, :]
                slope[b] = decay * (slope[b] + total[b])
                total[b] = decay * total[b] + g
                value[b % 2] = value[b % 2] + x * total[b]
                tilt[b % 2] = tilt[b % 2] + x * slope[b]
                state[b] = decay * (state[b] + earlier)
                lean[b] = decay * lean[b] + state[b]
        return total, slope, state, lean, value, tilt

    zero = jnp.zeros((POLES, LANES), jnp.float32)
    blank = [zero] * BLOCKS
    total, slope, state, lean, value, tilt = lax.fori_loop(
        0, BLOCK // UNROLL, steps, (blank, blank, blank, blank, [zero] * 2, [zero] * 2)
    )
    value = value[0] + value[1]
    tilt = tilt[0] + tilt[1]
    reach = jnp.exp(-float(BLOCK) * rate)
    coming, coming_slope = total[-1], slope[-1]
    behind, behind_lean = state[0], lean[0]
    for b in range(1, BLOCKS):
        back = BLOCKS - 1 - b
        value = value + state[back] * coming
        tilt = tilt + lean[back] * coming + state[back] * coming_slope
        coming_slope = slope[back] + reach * (coming_slope + float(BLOCK) * coming)
        coming = total[back] + reach * coming
        behind_lean = lean[b] + reach * (behind_lean + float(BLOCK) * behind)
        behind = state[b] + reach * behind
    low = low_half(zero.shape)
    turn = lambda v: pltpu.roll(v, CHANNELS, 1)
    late, late_slope = turn(coming), turn(coming_slope)
    value = value + jnp.where(low, behind * late, 0.0)
    tilt = tilt + jnp.where(low, behind_lean * late + behind * late_slope, 0.0)
    jump = jnp.exp(-float(HALF) * rate)
    sums = (
        coming + jump * late,
        coming_slope + jump * (late_slope + float(HALF) * late),
        jump * behind + turn(behind),
        jump * (behind_lean + float(HALF) * behind) + turn(behind_lean),
    )
    whole = [jnp.where(low, v, turn(v)) for v in sums] + [v + turn(v) for v in (value, tilt)]
    for q, v in enumerate(whole):
        rows_ref[q] = v
        packed = pack(rows_ref.at[q])
        for d in range(ROWS):
            msg_ref[d, pl.ds(q * SUBLANES, SUBLANES), :] = packed


def combine(recv_ref, rate, span, order):
    part = lambda d, q: recv_ref[order.index(d), pl.ds(q * SUBLANES, SUBLANES), :]
    decay = jnp.exp(-span * rate)
    coming = jnp.zeros_like(rate)
    coming_slope = jnp.zeros_like(rate)
    value = part(ROWS - 1, 4)
    tilt = part(ROWS - 1, 5)
    arriving = [coming] * ROWS
    for d in reversed(range(ROWS - 1)):
        coming_slope = part(d + 1, 1) + decay * (coming_slope + span * coming)
        coming = part(d + 1, 0) + decay * coming
        arriving[d] = coming
        value = value + part(d, 4) + part(d, 2) * coming
        tilt = tilt + part(d, 5) + part(d, 3) * coming + part(d, 2) * coming_slope
    slope = part(0, 1) + decay * (coming_slope + span * coming)
    total = part(0, 0) + decay * coming
    state = part(0, 2)
    lean = part(0, 3)
    for d in range(1, ROWS):
        lean = part(d, 3) + decay * (lean + span * state)
        state = part(d, 2) + decay * state
    return total, slope, state, lean, value, tilt, arriving


def pick(at, choices):
    out = choices[0]
    for d in range(1, ROWS):
        out = jnp.where(at == d, choices[d], out)
    return out


def row_kernel(at_ref, recv_ref, rate_ref, msg_ref, arrive_ref):
    rate = rate_ref[...]
    *sums, arriving = combine(recv_ref, rate, float(CHUNK), ROW_ORDER)
    for q, packed in enumerate(sums):
        for d in range(ROWS):
            msg_ref[d, pl.ds(q * SUBLANES, SUBLANES), :] = packed
    arrive_ref[...] = pick(lax.rem(at_ref[0], ROWS), arriving)


def column_kernel(at_ref, recv_ref, rate_ref, arrive_ref, msg_ref, state_ref):
    rate = rate_ref[...]
    sums = combine(recv_ref, rate, float(CHUNK * ROWS), COLUMN_ORDER)
    for q in range(2):
        for d in range(GROUP):
            msg_ref[d, pl.ds(q * SUBLANES, SUBLANES), :] = sums[4 + q]
    after = float(CHUNK) * (ROWS - 1 - lax.rem(at_ref[0], ROWS)).astype(jnp.float32)
    state_ref[...] = arrive_ref[...] + jnp.exp(-after * rate) * pick(lax.div(at_ref[0], ROWS), sums[6])


def post_kernel(gt_ref, rate_ref, weight_ref, state_ref, out_ref, yt_ref):
    full = (SUBLANES, LANES)
    low = low_half(full)
    low_row = low_half((1, LANES))
    block = lax.broadcasted_iota(jnp.int32, full, 0)
    after = float(STEP) * (SUBLANES - 1 - block).astype(jnp.float32)
    away = jnp.where(low, after + float(HALF), after)
    rates = double(rate_ref[...])
    weights = double(weight_ref[...])
    decays = jnp.exp(-rates)
    spans = jnp.exp(-float(STEP) * rates)
    wide = lambda rows, k: jnp.broadcast_to(rows[k : k + 1], full)
    for first in range(0, POLES, 8):
        poles = range(first, first + 8)
        decay = [wide(decays, k) for k in poles]

        def ends(at, total):
            g = gt_ref[pl.ds(STEP - 1 - at, SUBLANES, stride=STEP), :]
            return [decay[i] * total[i] + g for i in range(8)]

        blank = [jnp.zeros(full, jnp.float32)] * 8
        local = lax.fori_loop(0, STEP, ends, blank, unroll=POSTU)
        entry = []
        for i, k in enumerate(poles):
            total = local[i]
            far = wide(spans, k)
            for shift in (1, 2, 4):
                moved = pltpu.roll(total, SUBLANES - shift, 0)
                total = total + jnp.where(block < SUBLANES - shift, far * moved, 0.0)
                far = far * far
            inside = jnp.where(block < SUBLANES - 1, pltpu.roll(total, SUBLANES - 1, 0), 0.0)
            late = jnp.where(low, pltpu.roll(jnp.broadcast_to(total[0:1], full), CHANNELS, 1), 0.0)
            row = state_ref[pl.ds(k // 2, 1), :]
            other = pltpu.roll(row, CHANNELS, 1)
            both = jnp.where(low_row, row, other) if k % 2 == 0 else jnp.where(low_row, other, row)
            rate = rates[k : k + 1]
            entry.append(inside + jnp.exp(-after * rate) * late + jnp.exp(-away * rate) * both)
        weight = [wide(weights, k) for k in poles]

        def outputs(at, total):
            rows = pl.ds(STEP - 1 - at, SUBLANES, stride=STEP)
            g = gt_ref[rows, :]
            total = [decay[i] * total[i] + g for i in range(8)]
            terms = [weight[i] * total[i] for i in range(8)]
            while len(terms) > 1:
                terms = [terms[i] + terms[i + 1] for i in range(0, len(terms), 2)]
            yt_ref[rows, :] = terms[0] if first == 0 else yt_ref[rows, :] + terms[0]
            return total

        lax.fori_loop(0, STEP, outputs, entry, unroll=POSTU)
    stacked = yt_ref[...].T
    out_ref[:, :HALF] = stacked[:CHANNELS].astype(jnp.bfloat16)
    out_ref[:, HALF:] = stacked[CHANNELS:].astype(jnp.bfloat16)


def final_kernel(recv_ref, one_ref, two_ref, three_ref, res_ref, log_ref):
    value = recv_ref[0, pl.ds(0, SUBLANES), :]
    tilt = recv_ref[0, pl.ds(SUBLANES, SUBLANES), :]
    for d in range(1, GROUP):
        value = value + recv_ref[d, pl.ds(0, SUBLANES), :]
        tilt = tilt + recv_ref[d, pl.ds(SUBLANES, SUBLANES), :]
    for k in range(POLES):
        lanes = slice(0, CHANNELS) if k % 2 == 0 else slice(CHANNELS, LANES)
        first = value[k // 2 : k // 2 + 1, lanes]
        second = tilt[k // 2 : k // 2 + 1, lanes]
        at = pl.ds(k, 1)
        res_ref[at, :] = one_ref[at, :] * first
        log_ref[at, :] = two_ref[at, :] * first - three_ref[at, :] * second


def vmem(count):
    return [pl.BlockSpec(memory_space=pltpu.VMEM)] * count


def f32(*shape):
    return jax.ShapeDtypeStruct(shape, jnp.float32)


def scratch(*shape):
    return pltpu.VMEM(shape, jnp.float32)


def first_call(at, x, g, rate, name="pre"):
    return pl.pallas_call(
        pre_kernel,
        out_shape=(f32(ROWS, 6 * SUBLANES, LANES), f32(HALF, LANES), f32(SUBLANES, LANES)),
        in_specs=[pl.BlockSpec(memory_space=pltpu.SMEM)] + [pl.BlockSpec(memory_space=pltpu.HBM)] * 3,
        out_specs=tuple(vmem(3)),
        scratch_shapes=[
            pltpu.VMEM((CHANNELS, CHUNK), jnp.bfloat16),
            pltpu.VMEM((CHANNELS, CHUNK), jnp.bfloat16),
            scratch(POLES, CHANNELS),
            scratch(HALF, LANES),
            scratch(6, POLES, LANES),
            pltpu.SemaphoreType.DMA((3,)),
        ],
        compiler_params=GRANT,
        name=name,
    )(at, x, g, rate)


def body(inputs, grad_out, decay_rates, residues):
    rate = decay_rates.T
    residue = residues.T
    at = lax.axis_index("context").astype(jnp.int32).reshape(1)
    rows = [[y * ROWS + z for z in ROW_ORDER] for y in range(ROWS)]
    columns = [[y * ROWS + z for y in COLUMN_ORDER] for z in range(ROWS)]
    smem = [pl.BlockSpec(memory_space=pltpu.SMEM)]

    message, turned, packed = first_call(
        at, *(pltpu.with_memory_space_constraint(v, pltpu.HBM) for v in (inputs, grad_out, rate))
    )
    received = lax.all_to_all(message, "context", 0, 0, axis_index_groups=rows, tiled=True)
    message, arrived = pl.pallas_call(
        row_kernel,
        out_shape=(f32(ROWS, 6 * SUBLANES, LANES), f32(SUBLANES, LANES)),
        in_specs=smem + vmem(2),
        out_specs=tuple(vmem(2)),
        compiler_params=GRANT,
        name="row",
    )(at, received, packed)
    received = lax.all_to_all(message, "context", 0, 0, axis_index_groups=columns, tiled=True)
    message, state = pl.pallas_call(
        column_kernel,
        out_shape=(f32(GROUP, 2 * SUBLANES, LANES), f32(SUBLANES, LANES)),
        in_specs=smem + vmem(3),
        out_specs=tuple(vmem(2)),
        compiler_params=GRANT,
        name="column",
    )(at, received, packed, arrived)
    received = lax.all_to_all(message, "channel", 0, 0, axis_index_groups=[CHANNEL_ORDER], tiled=True)

    gain = jnp.sqrt(-jnp.expm1(-2.0 * rate))
    decay = jnp.exp(-rate)
    grad_in = pl.pallas_call(
        post_kernel,
        out_shape=jax.ShapeDtypeStruct((CHANNELS, CHUNK), jnp.bfloat16),
        in_specs=vmem(4),
        out_specs=vmem(1)[0],
        scratch_shapes=[scratch(HALF, LANES)],
        compiler_params=GRANT,
        name="post",
    )(turned, rate, residue * gain, state)
    norm = 1.0 / math.sqrt(CHUNK * ROWS * ROWS * GROUP)
    scaled = residue * rate * norm
    res_grad, log_grad = pl.pallas_call(
        final_kernel,
        out_shape=(f32(POLES, CHANNELS), f32(POLES, CHANNELS)),
        in_specs=vmem(4),
        out_specs=tuple(vmem(2)),
        compiler_params=GRANT,
        name="final",
    )(received, gain * norm, scaled * (decay * decay / gain), scaled * gain)
    return (grad_in, res_grad.T, log_grad.T)


def solution(mesh):
    return jax.shard_map(
        body,
        mesh=mesh,
        in_specs=(P("channel", "context"), P("channel", "context"), P(), P()),
        out_specs=(P("channel", "context"), P(), P()),
        check_vma=False,
    )
```

```python
import functools
import math

import jax
import jax.numpy as jnp
from jax import lax
from jax.experimental import pallas as pl
from jax.experimental.pallas import tpu as pltpu
from jax.sharding import PartitionSpec as P

LANES = 128
SUBLANES = 8
CHANNELS = 64
POLES = 16
STEP = 32
HALF = SUBLANES * STEP
CHUNK = 2 * HALF
BLOCKS = 8
BLOCK = HALF // BLOCKS
UNROLL = 16
POSTU = 32
ROWS = 8
GROUP = 8
ROW_ORDER = [6, 5, 4, 3, 2, 1, 0, 7]
COLUMN_ORDER = [4, 5, 3, 2, 0, 1, 7, 6]
CHANNEL_ORDER = [5, 7, 1, 3, 4, 6, 0, 2]
GRANT = pltpu.CompilerParams(vmem_limit_bytes=8 << 20)


def low_half(shape):
    return lax.broadcasted_iota(jnp.int32, shape, len(shape) - 1) < CHANNELS


def double(rows):
    return jnp.concatenate([rows, rows], axis=1)


def pack(ref):
    even = ref[pl.ds(0, SUBLANES, stride=2), :]
    odd = ref[pl.ds(1, SUBLANES, stride=2), :]
    return jnp.where(low_half(even.shape), even, odd)


def transposed(block):
    stacked = jnp.concatenate([block[:, :HALF], block[:, HALF:]], axis=0)
    return stacked.astype(jnp.float32).T


def pre_kernel(_, x_hbm, g_hbm, rate_hbm, msg_ref, gt_ref, packed_ref, entry_ref, x_ref, g_ref, rate_ref, xt_ref, rows_ref, sems):
    copies = [
        pltpu.make_async_copy(source, target, sems.at[i])
        for i, (source, target) in enumerate(((rate_hbm, rate_ref), (g_hbm, g_ref), (x_hbm, x_ref)))
    ]
    for copy in copies:
        copy.start()
    copies[0].wait()
    rate = double(rate_ref[...])
    rows_ref[0] = rate
    packed_ref[...] = pack(rows_ref.at[0])
    decay = jnp.exp(-rate)
    copies[1].wait()
    gt_ref[...] = transposed(g_ref[...])
    copies[2].wait()
    xt_ref[...] = transposed(x_ref[...])

    def steps(outer, carry):
        total, slope, state, lean, value, tilt = (list(part) for part in carry)
        for inner in range(UNROLL):
            for b in range(BLOCKS):
                up = pl.ds(b * BLOCK + outer * UNROLL + inner, 1)
                down = pl.ds((b + 1) * BLOCK - 1 - outer * UNROLL - inner, 1)
                g, x, earlier = gt_ref[down, :], xt_ref[down, :], xt_ref[up, :]
                slope[b] = decay * (slope[b] + total[b])
                total[b] = decay * total[b] + g
                value[b % 2] = value[b % 2] + x * total[b]
                tilt[b % 2] = tilt[b % 2] + x * slope[b]
                state[b] = decay * (state[b] + earlier)
                lean[b] = decay * lean[b] + state[b]
        return total, slope, state, lean, value, tilt

    zero = jnp.zeros((POLES, LANES), jnp.float32)
    blank = [zero] * BLOCKS
    total, slope, state, lean, value, tilt = lax.fori_loop(
        0, BLOCK // UNROLL, steps, (blank, blank, blank, blank, [zero] * 2, [zero] * 2)
    )
    value = value[0] + value[1]
    tilt = tilt[0] + tilt[1]
    reach = jnp.exp(-float(BLOCK) * rate)
    coming, coming_slope = total[-1], slope[-1]
    behind, behind_lean = state[0], lean[0]
    enter = [zero] * BLOCKS
    for b in range(1, BLOCKS):
        back = BLOCKS - 1 - b
        enter[back] = coming
        value = value + state[back] * coming
        tilt = tilt + lean[back] * coming + state[back] * coming_slope
        coming_slope = slope[back] + reach * (coming_slope + float(BLOCK) * coming)
        coming = total[back] + reach * coming
        behind_lean = lean[b] + reach * (behind_lean + float(BLOCK) * behind)
        behind = state[b] + reach * behind
    low = low_half(zero.shape)
    turn = lambda v: pltpu.roll(v, CHANNELS, 1)
    late, late_slope = turn(coming), turn(coming_slope)
    passing = jnp.where(low, late, 0.0)
    for b in reversed(range(BLOCKS)):
        entry_ref[pl.ds(b * POLES, POLES), :] = enter[b] + passing
        passing = reach * passing
    value = value + jnp.where(low, behind * late, 0.0)
    tilt = tilt + jnp.where(low, behind_lean * late + behind * late_slope, 0.0)
    jump = jnp.exp(-float(HALF) * rate)
    sums = (
        coming + jump * late,
        coming_slope + jump * (late_slope + float(HALF) * late),
        jump * behind + turn(behind),
        jump * (behind_lean + float(HALF) * behind) + turn(behind_lean),
    )
    whole = [jnp.where(low, v, turn(v)) for v in sums] + [v + turn(v) for v in (value, tilt)]
    for q, v in enumerate(whole):
        rows_ref[q] = v
        packed = pack(rows_ref.at[q])
        for d in range(ROWS):
            msg_ref[d, pl.ds(q * SUBLANES, SUBLANES), :] = packed


def combine(recv_ref, rate, span, order):
    part = lambda d, q: recv_ref[order.index(d), pl.ds(q * SUBLANES, SUBLANES), :]
    decay = jnp.exp(-span * rate)
    coming = jnp.zeros_like(rate)
    coming_slope = jnp.zeros_like(rate)
    value = part(ROWS - 1, 4)
    tilt = part(ROWS - 1, 5)
    arriving = [coming] * ROWS
    for d in reversed(range(ROWS - 1)):
        coming_slope = part(d + 1, 1) + decay * (coming_slope + span * coming)
        coming = part(d + 1, 0) + decay * coming
        arriving[d] = coming
        value = value + part(d, 4) + part(d, 2) * coming
        tilt = tilt + part(d, 5) + part(d, 3) * coming + part(d, 2) * coming_slope
    slope = part(0, 1) + decay * (coming_slope + span * coming)
    total = part(0, 0) + decay * coming
    state = part(0, 2)
    lean = part(0, 3)
    for d in range(1, ROWS):
        lean = part(d, 3) + decay * (lean + span * state)
        state = part(d, 2) + decay * state
    return total, slope, state, lean, value, tilt, arriving


def pick(at, choices):
    out = choices[0]
    for d in range(1, ROWS):
        out = jnp.where(at == d, choices[d], out)
    return out


def row_kernel(at_ref, recv_ref, rate_ref, msg_ref, arrive_ref):
    rate = rate_ref[...]
    *sums, arriving = combine(recv_ref, rate, float(CHUNK), ROW_ORDER)
    for q, packed in enumerate(sums):
        for d in range(ROWS):
            msg_ref[d, pl.ds(q * SUBLANES, SUBLANES), :] = packed
    arrive_ref[...] = pick(lax.rem(at_ref[0], ROWS), arriving)


def column_kernel(at_ref, recv_ref, rate_ref, arrive_ref, msg_ref, state_ref):
    rate = rate_ref[...]
    sums = combine(recv_ref, rate, float(CHUNK * ROWS), COLUMN_ORDER)
    for q in range(2):
        for d in range(GROUP):
            msg_ref[d, pl.ds(q * SUBLANES, SUBLANES), :] = sums[4 + q]
    after = float(CHUNK) * (ROWS - 1 - lax.rem(at_ref[0], ROWS)).astype(jnp.float32)
    state_ref[...] = arrive_ref[...] + jnp.exp(-after * rate) * pick(lax.div(at_ref[0], ROWS), sums[6])


def last_kernel(gt_ref, entry_ref, rate_ref, weight_ref, state_ref, recv_ref, one_ref, two_ref, three_ref, out_ref, res_ref, log_ref, yt_ref):
    final_kernel(recv_ref, one_ref, two_ref, three_ref, res_ref, log_ref)
    post_kernel(gt_ref, entry_ref, rate_ref, weight_ref, state_ref, out_ref, yt_ref)


def post_kernel(gt_ref, entry_ref, rate_ref, weight_ref, state_ref, out_ref, yt_ref):
    full = (SUBLANES, LANES)
    low = low_half(full)
    low_row = low_half((1, LANES))
    block = lax.broadcasted_iota(jnp.int32, full, 0)
    after = float(STEP) * (SUBLANES - 1 - block).astype(jnp.float32)
    away = jnp.where(low, after + float(HALF), after)
    rates = double(rate_ref[...])
    weights = double(weight_ref[...])
    decays = jnp.exp(-rates)
    wide = lambda rows, k: jnp.broadcast_to(rows[k : k + 1], full)
    for first in range(0, POLES, 8):
        poles = range(first, first + 8)
        decay = [wide(decays, k) for k in poles]

        entry = []
        for k in poles:
            row = state_ref[pl.ds(k // 2, 1), :]
            other = pltpu.roll(row, CHANNELS, 1)
            both = jnp.where(low_row, row, other) if k % 2 == 0 else jnp.where(low_row, other, row)
            entry.append(entry_ref[pl.ds(k, SUBLANES, stride=POLES), :] + jnp.exp(-away * rates[k : k + 1]) * both)
        weight = [wide(weights, k) for k in poles]

        def outputs(at, total):
            rows = pl.ds(STEP - 1 - at, SUBLANES, stride=STEP)
            g = gt_ref[rows, :]
            total = [decay[i] * total[i] + g for i in range(8)]
            terms = [weight[i] * total[i] for i in range(8)]
            while len(terms) > 1:
                terms = [terms[i] + terms[i + 1] for i in range(0, len(terms), 2)]
            yt_ref[rows, :] = terms[0] if first == 0 else yt_ref[rows, :] + terms[0]
            return total

        lax.fori_loop(0, STEP, outputs, entry, unroll=POSTU)
    stacked = yt_ref[...].T
    out_ref[:, :HALF] = stacked[:CHANNELS].astype(jnp.bfloat16)
    out_ref[:, HALF:] = stacked[CHANNELS:].astype(jnp.bfloat16)


def final_kernel(recv_ref, one_ref, two_ref, three_ref, res_ref, log_ref):
    value = recv_ref[0, pl.ds(0, SUBLANES), :]
    tilt = recv_ref[0, pl.ds(SUBLANES, SUBLANES), :]
    for d in range(1, GROUP):
        value = value + recv_ref[d, pl.ds(0, SUBLANES), :]
        tilt = tilt + recv_ref[d, pl.ds(SUBLANES, SUBLANES), :]
    for k in range(POLES):
        lanes = slice(0, CHANNELS) if k % 2 == 0 else slice(CHANNELS, LANES)
        first = value[k // 2 : k // 2 + 1, lanes]
        second = tilt[k // 2 : k // 2 + 1, lanes]
        at = pl.ds(k, 1)
        res_ref[at, :] = one_ref[at, :] * first
        log_ref[at, :] = two_ref[at, :] * first - three_ref[at, :] * second


def vmem(count):
    return [pl.BlockSpec(memory_space=pltpu.VMEM)] * count


def f32(*shape):
    return jax.ShapeDtypeStruct(shape, jnp.float32)


def scratch(*shape):
    return pltpu.VMEM(shape, jnp.float32)


def first_call(at, x, g, rate, name="pre"):
    return pl.pallas_call(
        pre_kernel,
        out_shape=(f32(ROWS, 6 * SUBLANES, LANES), f32(HALF, LANES), f32(SUBLANES, LANES), f32(LANES, LANES)),
        in_specs=[pl.BlockSpec(memory_space=pltpu.SMEM)] + [pl.BlockSpec(memory_space=pltpu.HBM)] * 3,
        out_specs=tuple(vmem(4)),
        scratch_shapes=[
            pltpu.VMEM((CHANNELS, CHUNK), jnp.bfloat16),
            pltpu.VMEM((CHANNELS, CHUNK), jnp.bfloat16),
            scratch(POLES, CHANNELS),
            scratch(HALF, LANES),
            scratch(6, POLES, LANES),
            pltpu.SemaphoreType.DMA((3,)),
        ],
        compiler_params=GRANT,
        name=name,
    )(at, x, g, rate)


def body(inputs, grad_out, decay_rates, residues):
    rate = decay_rates.T
    residue = residues.T
    at = lax.axis_index("context").astype(jnp.int32).reshape(1)
    rows = [[y * ROWS + z for z in ROW_ORDER] for y in range(ROWS)]
    columns = [[y * ROWS + z for y in COLUMN_ORDER] for z in range(ROWS)]
    smem = [pl.BlockSpec(memory_space=pltpu.SMEM)]

    message, turned, packed, entry = first_call(
        at, *(pltpu.with_memory_space_constraint(v, pltpu.HBM) for v in (inputs, grad_out, rate))
    )
    received = lax.all_to_all(message, "context", 0, 0, axis_index_groups=rows, tiled=True)
    message, arrived = pl.pallas_call(
        row_kernel,
        out_shape=(f32(ROWS, 6 * SUBLANES, LANES), f32(SUBLANES, LANES)),
        in_specs=smem + vmem(2),
        out_specs=tuple(vmem(2)),
        compiler_params=GRANT,
        name="row",
    )(at, received, packed)
    received = lax.all_to_all(message, "context", 0, 0, axis_index_groups=columns, tiled=True)
    message, state = pl.pallas_call(
        column_kernel,
        out_shape=(f32(GROUP, 2 * SUBLANES, LANES), f32(SUBLANES, LANES)),
        in_specs=smem + vmem(3),
        out_specs=tuple(vmem(2)),
        compiler_params=GRANT,
        name="column",
    )(at, received, packed, arrived)
    received = lax.all_to_all(message, "channel", 0, 0, axis_index_groups=[CHANNEL_ORDER], tiled=True)

    received, rate, residue = lax.optimization_barrier((received, rate, residue))
    gain = jnp.sqrt(-jnp.expm1(-2.0 * rate))
    decay = jnp.exp(-rate)
    norm = 1.0 / math.sqrt(CHUNK * ROWS * ROWS * GROUP)
    scaled = residue * rate * norm
    grad_in, res_grad, log_grad = pl.pallas_call(
        last_kernel,
        out_shape=(jax.ShapeDtypeStruct((CHANNELS, CHUNK), jnp.bfloat16), f32(POLES, CHANNELS), f32(POLES, CHANNELS)),
        in_specs=vmem(9),
        out_specs=tuple(vmem(3)),
        scratch_shapes=[scratch(HALF, LANES)],
        compiler_params=GRANT,
        name="last",
    )(turned, entry, rate, residue * gain, state, received, gain * norm, scaled * (decay * decay / gain), scaled * gain)
    return (grad_in, res_grad.T, log_grad.T)


def solution(mesh):
    return jax.shard_map(
        body,
        mesh=mesh,
        in_specs=(P("channel", "context"), P("channel", "context"), P(), P()),
        out_specs=(P("channel", "context"), P(), P()),
        check_vma=False,
    )
```

```python
import functools
import math

import jax
import jax.numpy as jnp
from jax import lax
from jax.experimental import pallas as pl
from jax.experimental.pallas import tpu as pltpu
from jax.sharding import PartitionSpec as P

LANES = 128
SUBLANES = 8
CHANNELS = 64
POLES = 16
STEP = 32
HALF = SUBLANES * STEP
CHUNK = 2 * HALF
BLOCKS = 8
BLOCK = HALF // BLOCKS
UNROLL = 16
POSTU = 32
WIDTH = 16
ROWS = 8
GROUP = 8
ROW_ORDER = [6, 5, 4, 3, 2, 1, 0, 7]
COLUMN_ORDER = [4, 5, 3, 2, 0, 1, 7, 6]
CHANNEL_ORDER = [5, 7, 1, 3, 4, 6, 0, 2]
GRANT = pltpu.CompilerParams(vmem_limit_bytes=8 << 20)


def low_half(shape):
    return lax.broadcasted_iota(jnp.int32, shape, len(shape) - 1) < CHANNELS


def double(rows):
    return jnp.concatenate([rows, rows], axis=1)


def pack(ref):
    even = ref[pl.ds(0, SUBLANES, stride=2), :]
    odd = ref[pl.ds(1, SUBLANES, stride=2), :]
    return jnp.where(low_half(even.shape), even, odd)


def transposed(block):
    stacked = jnp.concatenate([block[:, :HALF], block[:, HALF:]], axis=0)
    return stacked.astype(jnp.float32).T


def pre_kernel(_, x_hbm, g_hbm, rate_hbm, msg_ref, gt_ref, packed_ref, entry_ref, x_ref, g_ref, rate_ref, xt_ref, rows_ref, sems):
    copies = [
        pltpu.make_async_copy(source, target, sems.at[i])
        for i, (source, target) in enumerate(((rate_hbm, rate_ref), (g_hbm, g_ref), (x_hbm, x_ref)))
    ]
    for copy in copies:
        copy.start()
    copies[0].wait()
    rate = double(rate_ref[...])
    rows_ref[0] = rate
    packed_ref[...] = pack(rows_ref.at[0])
    decay = jnp.exp(-rate)
    copies[1].wait()
    gt_ref[...] = transposed(g_ref[...])
    copies[2].wait()
    xt_ref[...] = transposed(x_ref[...])

    def steps(outer, carry):
        total, slope, state, lean, value, tilt = (list(part) for part in carry)
        for inner in range(UNROLL):
            for b in range(BLOCKS):
                up = pl.ds(b * BLOCK + outer * UNROLL + inner, 1)
                down = pl.ds((b + 1) * BLOCK - 1 - outer * UNROLL - inner, 1)
                g, x, earlier = gt_ref[down, :], xt_ref[down, :], xt_ref[up, :]
                slope[b] = decay * (slope[b] + total[b])
                total[b] = decay * total[b] + g
                value[b % 2] = value[b % 2] + x * total[b]
                tilt[b % 2] = tilt[b % 2] + x * slope[b]
                state[b] = decay * (state[b] + earlier)
                lean[b] = decay * lean[b] + state[b]
        return total, slope, state, lean, value, tilt

    zero = jnp.zeros((POLES, LANES), jnp.float32)
    blank = [zero] * BLOCKS
    total, slope, state, lean, value, tilt = lax.fori_loop(
        0, BLOCK // UNROLL, steps, (blank, blank, blank, blank, [zero] * 2, [zero] * 2)
    )
    value = value[0] + value[1]
    tilt = tilt[0] + tilt[1]
    reach = jnp.exp(-float(BLOCK) * rate)
    coming, coming_slope = total[-1], slope[-1]
    behind, behind_lean = state[0], lean[0]
    enter = [zero] * BLOCKS
    for b in range(1, BLOCKS):
        back = BLOCKS - 1 - b
        enter[back] = coming
        value = value + state[back] * coming
        tilt = tilt + lean[back] * coming + state[back] * coming_slope
        coming_slope = slope[back] + reach * (coming_slope + float(BLOCK) * coming)
        coming = total[back] + reach * coming
        behind_lean = lean[b] + reach * (behind_lean + float(BLOCK) * behind)
        behind = state[b] + reach * behind
    low = low_half(zero.shape)
    turn = lambda v: pltpu.roll(v, CHANNELS, 1)
    late, late_slope = turn(coming), turn(coming_slope)
    passing = jnp.where(low, late, 0.0)
    for b in reversed(range(BLOCKS)):
        entry_ref[pl.ds(b * POLES, POLES), :] = enter[b] + passing
        passing = reach * passing
    value = value + jnp.where(low, behind * late, 0.0)
    tilt = tilt + jnp.where(low, behind_lean * late + behind * late_slope, 0.0)
    jump = jnp.exp(-float(HALF) * rate)
    sums = (
        coming + jump * late,
        coming_slope + jump * (late_slope + float(HALF) * late),
        jump * behind + turn(behind),
        jump * (behind_lean + float(HALF) * behind) + turn(behind_lean),
    )
    whole = [jnp.where(low, v, turn(v)) for v in sums] + [v + turn(v) for v in (value, tilt)]
    for q, v in enumerate(whole):
        rows_ref[q] = v
        packed = pack(rows_ref.at[q])
        for d in range(ROWS):
            msg_ref[d, pl.ds(q * SUBLANES, SUBLANES), :] = packed


def combine(recv_ref, rate, span, order):
    part = lambda d, q: recv_ref[order.index(d), pl.ds(q * SUBLANES, SUBLANES), :]
    decay = jnp.exp(-span * rate)
    coming = jnp.zeros_like(rate)
    coming_slope = jnp.zeros_like(rate)
    value = part(ROWS - 1, 4)
    tilt = part(ROWS - 1, 5)
    arriving = [coming] * ROWS
    for d in reversed(range(ROWS - 1)):
        coming_slope = part(d + 1, 1) + decay * (coming_slope + span * coming)
        coming = part(d + 1, 0) + decay * coming
        arriving[d] = coming
        value = value + part(d, 4) + part(d, 2) * coming
        tilt = tilt + part(d, 5) + part(d, 3) * coming + part(d, 2) * coming_slope
    slope = part(0, 1) + decay * (coming_slope + span * coming)
    total = part(0, 0) + decay * coming
    state = part(0, 2)
    lean = part(0, 3)
    for d in range(1, ROWS):
        lean = part(d, 3) + decay * (lean + span * state)
        state = part(d, 2) + decay * state
    return total, slope, state, lean, value, tilt, arriving


def pick(at, choices):
    out = choices[0]
    for d in range(1, ROWS):
        out = jnp.where(at == d, choices[d], out)
    return out


def row_kernel(at_ref, recv_ref, rate_ref, msg_ref, arrive_ref):
    rate = rate_ref[...]
    *sums, arriving = combine(recv_ref, rate, float(CHUNK), ROW_ORDER)
    for q, packed in enumerate(sums):
        for d in range(ROWS):
            msg_ref[d, pl.ds(q * SUBLANES, SUBLANES), :] = packed
    arrive_ref[...] = pick(lax.rem(at_ref[0], ROWS), arriving)


def column_kernel(at_ref, recv_ref, rate_ref, arrive_ref, msg_ref, state_ref):
    rate = rate_ref[...]
    sums = combine(recv_ref, rate, float(CHUNK * ROWS), COLUMN_ORDER)
    for q in range(2):
        for d in range(GROUP):
            msg_ref[d, pl.ds(q * SUBLANES, SUBLANES), :] = sums[4 + q]
    after = float(CHUNK) * (ROWS - 1 - lax.rem(at_ref[0], ROWS)).astype(jnp.float32)
    state_ref[...] = arrive_ref[...] + jnp.exp(-after * rate) * pick(lax.div(at_ref[0], ROWS), sums[6])


def last_kernel(gt_ref, entry_ref, rate_ref, weight_ref, state_ref, recv_ref, one_ref, two_ref, three_ref, out_ref, res_ref, log_ref, yt_ref):
    final_kernel(recv_ref, one_ref, two_ref, three_ref, res_ref, log_ref)
    post_kernel(gt_ref, entry_ref, rate_ref, weight_ref, state_ref, out_ref, yt_ref)


def post_kernel(gt_ref, entry_ref, rate_ref, weight_ref, state_ref, out_ref, yt_ref):
    full = (SUBLANES, LANES)
    low = low_half(full)
    low_row = low_half((1, LANES))
    block = lax.broadcasted_iota(jnp.int32, full, 0)
    after = float(STEP) * (SUBLANES - 1 - block).astype(jnp.float32)
    away = jnp.where(low, after + float(HALF), after)
    rates = double(rate_ref[...])
    weights = double(weight_ref[...])
    decays = jnp.exp(-rates)
    wide = lambda rows, k: jnp.broadcast_to(rows[k : k + 1], full)
    for first in range(0, POLES, WIDTH):
        poles = range(first, first + WIDTH)
        decay = [wide(decays, k) for k in poles]

        entry = []
        for k in poles:
            row = state_ref[pl.ds(k // 2, 1), :]
            other = pltpu.roll(row, CHANNELS, 1)
            both = jnp.where(low_row, row, other) if k % 2 == 0 else jnp.where(low_row, other, row)
            entry.append(entry_ref[pl.ds(k, SUBLANES, stride=POLES), :] + jnp.exp(-away * rates[k : k + 1]) * both)
        weight = [wide(weights, k) for k in poles]

        def outputs(at, total):
            rows = pl.ds(STEP - 1 - at, SUBLANES, stride=STEP)
            g = gt_ref[rows, :]
            total = [decay[i] * total[i] + g for i in range(WIDTH)]
            terms = [weight[i] * total[i] for i in range(WIDTH)]
            while len(terms) > 1:
                terms = [terms[i] + terms[i + 1] for i in range(0, len(terms), 2)]
            yt_ref[rows, :] = terms[0] if first == 0 else yt_ref[rows, :] + terms[0]
            return total

        lax.fori_loop(0, STEP, outputs, entry, unroll=POSTU)
    stacked = yt_ref[...].T
    out_ref[:, :HALF] = stacked[:CHANNELS].astype(jnp.bfloat16)
    out_ref[:, HALF:] = stacked[CHANNELS:].astype(jnp.bfloat16)


def final_kernel(recv_ref, one_ref, two_ref, three_ref, res_ref, log_ref):
    value = recv_ref[0, pl.ds(0, SUBLANES), :]
    tilt = recv_ref[0, pl.ds(SUBLANES, SUBLANES), :]
    for d in range(1, GROUP):
        value = value + recv_ref[d, pl.ds(0, SUBLANES), :]
        tilt = tilt + recv_ref[d, pl.ds(SUBLANES, SUBLANES), :]
    for k in range(POLES):
        lanes = slice(0, CHANNELS) if k % 2 == 0 else slice(CHANNELS, LANES)
        first = value[k // 2 : k // 2 + 1, lanes]
        second = tilt[k // 2 : k // 2 + 1, lanes]
        at = pl.ds(k, 1)
        res_ref[at, :] = one_ref[at, :] * first
        log_ref[at, :] = two_ref[at, :] * first - three_ref[at, :] * second


def vmem(count):
    return [pl.BlockSpec(memory_space=pltpu.VMEM)] * count


def f32(*shape):
    return jax.ShapeDtypeStruct(shape, jnp.float32)


def scratch(*shape):
    return pltpu.VMEM(shape, jnp.float32)


def first_call(at, x, g, rate, name="pre"):
    return pl.pallas_call(
        pre_kernel,
        out_shape=(f32(ROWS, 6 * SUBLANES, LANES), f32(HALF, LANES), f32(SUBLANES, LANES), f32(LANES, LANES)),
        in_specs=[pl.BlockSpec(memory_space=pltpu.SMEM)] + [pl.BlockSpec(memory_space=pltpu.HBM)] * 3,
        out_specs=tuple(vmem(4)),
        scratch_shapes=[
            pltpu.VMEM((CHANNELS, CHUNK), jnp.bfloat16),
            pltpu.VMEM((CHANNELS, CHUNK), jnp.bfloat16),
            scratch(POLES, CHANNELS),
            scratch(HALF, LANES),
            scratch(6, POLES, LANES),
            pltpu.SemaphoreType.DMA((3,)),
        ],
        compiler_params=GRANT,
        name=name,
    )(at, x, g, rate)


def body(inputs, grad_out, decay_rates, residues):
    rate = decay_rates.T
    residue = residues.T
    at = lax.axis_index("context").astype(jnp.int32).reshape(1)
    rows = [[y * ROWS + z for z in ROW_ORDER] for y in range(ROWS)]
    columns = [[y * ROWS + z for y in COLUMN_ORDER] for z in range(ROWS)]
    smem = [pl.BlockSpec(memory_space=pltpu.SMEM)]

    message, turned, packed, entry = first_call(
        at, *(pltpu.with_memory_space_constraint(v, pltpu.HBM) for v in (inputs, grad_out, rate))
    )
    received = lax.all_to_all(message, "context", 0, 0, axis_index_groups=rows, tiled=True)
    message, arrived = pl.pallas_call(
        row_kernel,
        out_shape=(f32(ROWS, 6 * SUBLANES, LANES), f32(SUBLANES, LANES)),
        in_specs=smem + vmem(2),
        out_specs=tuple(vmem(2)),
        compiler_params=GRANT,
        name="row",
    )(at, received, packed)
    received = lax.all_to_all(message, "context", 0, 0, axis_index_groups=columns, tiled=True)
    message, state = pl.pallas_call(
        column_kernel,
        out_shape=(f32(GROUP, 2 * SUBLANES, LANES), f32(SUBLANES, LANES)),
        in_specs=smem + vmem(3),
        out_specs=tuple(vmem(2)),
        compiler_params=GRANT,
        name="column",
    )(at, received, packed, arrived)
    received = lax.all_to_all(message, "channel", 0, 0, axis_index_groups=[CHANNEL_ORDER], tiled=True)

    received, rate, residue = lax.optimization_barrier((received, rate, residue))
    gain = jnp.sqrt(-jnp.expm1(-2.0 * rate))
    decay = jnp.exp(-rate)
    norm = 1.0 / math.sqrt(CHUNK * ROWS * ROWS * GROUP)
    scaled = residue * rate * norm
    grad_in, res_grad, log_grad = pl.pallas_call(
        last_kernel,
        out_shape=(jax.ShapeDtypeStruct((CHANNELS, CHUNK), jnp.bfloat16), f32(POLES, CHANNELS), f32(POLES, CHANNELS)),
        in_specs=vmem(9),
        out_specs=tuple(vmem(3)),
        scratch_shapes=[scratch(HALF, LANES)],
        compiler_params=GRANT,
        name="last",
    )(turned, entry, rate, residue * gain, state, received, gain * norm, scaled * (decay * decay / gain), scaled * gain)
    return (grad_in, res_grad.T, log_grad.T)


def solution(mesh):
    return jax.shard_map(
        body,
        mesh=mesh,
        in_specs=(P("channel", "context"), P("channel", "context"), P(), P()),
        out_specs=(P("channel", "context"), P(), P()),
        check_vma=False,
    )
```

```python
import functools
import math

import jax
import jax.numpy as jnp
from jax import lax
from jax.experimental import pallas as pl
from jax.experimental.pallas import tpu as pltpu
from jax.sharding import PartitionSpec as P

LANES = 128
SUBLANES = 8
CHANNELS = 64
POLES = 16
STEP = 32
HALF = SUBLANES * STEP
CHUNK = 2 * HALF
BLOCKS = 8
BLOCK = HALF // BLOCKS
UNROLL = 16
POSTU = 32
WIDTH = 16
ROWS = 8
GROUP = 8
ROW_ORDER = [6, 5, 4, 3, 2, 1, 0, 7]
COLUMN_ORDER = [4, 5, 3, 2, 0, 1, 7, 6]
CHANNEL_ORDER = [5, 7, 1, 3, 0, 2, 4, 6]
GRANT = pltpu.CompilerParams(vmem_limit_bytes=8 << 20)


def low_half(shape):
    return lax.broadcasted_iota(jnp.int32, shape, len(shape) - 1) < CHANNELS


def double(rows):
    return jnp.concatenate([rows, rows], axis=1)


def pack(ref):
    even = ref[pl.ds(0, SUBLANES, stride=2), :]
    odd = ref[pl.ds(1, SUBLANES, stride=2), :]
    return jnp.where(low_half(even.shape), even, odd)


def transposed(block):
    stacked = jnp.concatenate([block[:, :HALF], block[:, HALF:]], axis=0)
    return stacked.astype(jnp.float32).T


def pre_kernel(_, x_hbm, g_hbm, rate_hbm, msg_ref, gt_ref, packed_ref, entry_ref, x_ref, g_ref, rate_ref, xt_ref, rows_ref, sems):
    copies = [
        pltpu.make_async_copy(source, target, sems.at[i])
        for i, (source, target) in enumerate(((rate_hbm, rate_ref), (g_hbm, g_ref), (x_hbm, x_ref)))
    ]
    for copy in copies:
        copy.start()
    copies[0].wait()
    rate = double(rate_ref[...])
    rows_ref[0] = rate
    packed_ref[...] = pack(rows_ref.at[0])
    decay = jnp.exp(-rate)
    copies[1].wait()
    gt_ref[...] = transposed(g_ref[...])
    copies[2].wait()
    xt_ref[...] = transposed(x_ref[...])

    def steps(outer, carry):
        total, slope, state, lean, value, tilt = (list(part) for part in carry)
        for inner in range(UNROLL):
            for b in range(BLOCKS):
                up = pl.ds(b * BLOCK + outer * UNROLL + inner, 1)
                down = pl.ds((b + 1) * BLOCK - 1 - outer * UNROLL - inner, 1)
                g, x, earlier = gt_ref[down, :], xt_ref[down, :], xt_ref[up, :]
                slope[b] = decay * (slope[b] + total[b])
                total[b] = decay * total[b] + g
                value[b % 2] = value[b % 2] + x * total[b]
                tilt[b % 2] = tilt[b % 2] + x * slope[b]
                state[b] = decay * (state[b] + earlier)
                lean[b] = decay * lean[b] + state[b]
        return total, slope, state, lean, value, tilt

    zero = jnp.zeros((POLES, LANES), jnp.float32)
    blank = [zero] * BLOCKS
    total, slope, state, lean, value, tilt = lax.fori_loop(
        0, BLOCK // UNROLL, steps, (blank, blank, blank, blank, [zero] * 2, [zero] * 2)
    )
    value = value[0] + value[1]
    tilt = tilt[0] + tilt[1]
    reach = jnp.exp(-float(BLOCK) * rate)
    coming, coming_slope = total[-1], slope[-1]
    behind, behind_lean = state[0], lean[0]
    enter = [zero] * BLOCKS
    for b in range(1, BLOCKS):
        back = BLOCKS - 1 - b
        enter[back] = coming
        value = value + state[back] * coming
        tilt = tilt + lean[back] * coming + state[back] * coming_slope
        coming_slope = slope[back] + reach * (coming_slope + float(BLOCK) * coming)
        coming = total[back] + reach * coming
        behind_lean = lean[b] + reach * (behind_lean + float(BLOCK) * behind)
        behind = state[b] + reach * behind
    low = low_half(zero.shape)
    turn = lambda v: pltpu.roll(v, CHANNELS, 1)
    late, late_slope = turn(coming), turn(coming_slope)
    passing = jnp.where(low, late, 0.0)
    for b in reversed(range(BLOCKS)):
        entry_ref[pl.ds(b * POLES, POLES), :] = enter[b] + passing
        passing = reach * passing
    value = value + jnp.where(low, behind * late, 0.0)
    tilt = tilt + jnp.where(low, behind_lean * late + behind * late_slope, 0.0)
    jump = jnp.exp(-float(HALF) * rate)
    sums = (
        coming + jump * late,
        coming_slope + jump * (late_slope + float(HALF) * late),
        jump * behind + turn(behind),
        jump * (behind_lean + float(HALF) * behind) + turn(behind_lean),
    )
    whole = [jnp.where(low, v, turn(v)) for v in sums] + [v + turn(v) for v in (value, tilt)]
    for q, v in enumerate(whole):
        rows_ref[q] = v
        packed = pack(rows_ref.at[q])
        for d in range(ROWS):
            msg_ref[d, pl.ds(q * SUBLANES, SUBLANES), :] = packed


def combine(recv_ref, rate, span, order):
    part = lambda d, q: recv_ref[order.index(d), pl.ds(q * SUBLANES, SUBLANES), :]
    decay = jnp.exp(-span * rate)
    coming = jnp.zeros_like(rate)
    coming_slope = jnp.zeros_like(rate)
    value = part(ROWS - 1, 4)
    tilt = part(ROWS - 1, 5)
    arriving = [coming] * ROWS
    for d in reversed(range(ROWS - 1)):
        coming_slope = part(d + 1, 1) + decay * (coming_slope + span * coming)
        coming = part(d + 1, 0) + decay * coming
        arriving[d] = coming
        value = value + part(d, 4) + part(d, 2) * coming
        tilt = tilt + part(d, 5) + part(d, 3) * coming + part(d, 2) * coming_slope
    slope = part(0, 1) + decay * (coming_slope + span * coming)
    total = part(0, 0) + decay * coming
    state = part(0, 2)
    lean = part(0, 3)
    for d in range(1, ROWS):
        lean = part(d, 3) + decay * (lean + span * state)
        state = part(d, 2) + decay * state
    return total, slope, state, lean, value, tilt, arriving


def pick(at, choices):
    out = choices[0]
    for d in range(1, ROWS):
        out = jnp.where(at == d, choices[d], out)
    return out


def row_kernel(at_ref, recv_ref, rate_ref, msg_ref, arrive_ref):
    rate = rate_ref[...]
    *sums, arriving = combine(recv_ref, rate, float(CHUNK), ROW_ORDER)
    for q, packed in enumerate(sums):
        for d in range(ROWS):
            msg_ref[d, pl.ds(q * SUBLANES, SUBLANES), :] = packed
    arrive_ref[...] = pick(lax.rem(at_ref[0], ROWS), arriving)


def column_kernel(at_ref, recv_ref, rate_ref, arrive_ref, msg_ref, state_ref):
    rate = rate_ref[...]
    sums = combine(recv_ref, rate, float(CHUNK * ROWS), COLUMN_ORDER)
    for q in range(2):
        for d in range(GROUP):
            msg_ref[d, pl.ds(q * SUBLANES, SUBLANES), :] = sums[4 + q]
    after = float(CHUNK) * (ROWS - 1 - lax.rem(at_ref[0], ROWS)).astype(jnp.float32)
    state_ref[...] = arrive_ref[...] + jnp.exp(-after * rate) * pick(lax.div(at_ref[0], ROWS), sums[6])


def last_kernel(gt_ref, entry_ref, rate_ref, weight_ref, state_ref, recv_ref, one_ref, two_ref, three_ref, out_ref, res_ref, log_ref, yt_ref):
    final_kernel(recv_ref, one_ref, two_ref, three_ref, res_ref, log_ref)
    post_kernel(gt_ref, entry_ref, rate_ref, weight_ref, state_ref, out_ref, yt_ref)


def post_kernel(gt_ref, entry_ref, rate_ref, weight_ref, state_ref, out_ref, yt_ref):
    full = (SUBLANES, LANES)
    low = low_half(full)
    low_row = low_half((1, LANES))
    block = lax.broadcasted_iota(jnp.int32, full, 0)
    after = float(STEP) * (SUBLANES - 1 - block).astype(jnp.float32)
    away = jnp.where(low, after + float(HALF), after)
    rates = double(rate_ref[...])
    weights = double(weight_ref[...])
    decays = jnp.exp(-rates)
    wide = lambda rows, k: jnp.broadcast_to(rows[k : k + 1], full)
    for first in range(0, POLES, WIDTH):
        poles = range(first, first + WIDTH)
        decay = [wide(decays, k) for k in poles]

        entry = []
        for k in poles:
            row = state_ref[pl.ds(k // 2, 1), :]
            other = pltpu.roll(row, CHANNELS, 1)
            both = jnp.where(low_row, row, other) if k % 2 == 0 else jnp.where(low_row, other, row)
            entry.append(entry_ref[pl.ds(k, SUBLANES, stride=POLES), :] + jnp.exp(-away * rates[k : k + 1]) * both)
        weight = [wide(weights, k) for k in poles]

        def outputs(at, total):
            rows = pl.ds(STEP - 1 - at, SUBLANES, stride=STEP)
            g = gt_ref[rows, :]
            total = [decay[i] * total[i] + g for i in range(WIDTH)]
            terms = [weight[i] * total[i] for i in range(WIDTH)]
            while len(terms) > 1:
                terms = [terms[i] + terms[i + 1] for i in range(0, len(terms), 2)]
            yt_ref[rows, :] = terms[0] if first == 0 else yt_ref[rows, :] + terms[0]
            return total

        lax.fori_loop(0, STEP, outputs, entry, unroll=POSTU)
    stacked = yt_ref[...].T
    out_ref[:, :HALF] = stacked[:CHANNELS].astype(jnp.bfloat16)
    out_ref[:, HALF:] = stacked[CHANNELS:].astype(jnp.bfloat16)


def final_kernel(recv_ref, one_ref, two_ref, three_ref, res_ref, log_ref):
    value = recv_ref[0, pl.ds(0, SUBLANES), :]
    tilt = recv_ref[0, pl.ds(SUBLANES, SUBLANES), :]
    for d in range(1, GROUP):
        value = value + recv_ref[d, pl.ds(0, SUBLANES), :]
        tilt = tilt + recv_ref[d, pl.ds(SUBLANES, SUBLANES), :]
    for k in range(POLES):
        lanes = slice(0, CHANNELS) if k % 2 == 0 else slice(CHANNELS, LANES)
        first = value[k // 2 : k // 2 + 1, lanes]
        second = tilt[k // 2 : k // 2 + 1, lanes]
        at = pl.ds(k, 1)
        res_ref[at, :] = one_ref[at, :] * first
        log_ref[at, :] = two_ref[at, :] * first - three_ref[at, :] * second


def vmem(count):
    return [pl.BlockSpec(memory_space=pltpu.VMEM)] * count


def f32(*shape):
    return jax.ShapeDtypeStruct(shape, jnp.float32)


def scratch(*shape):
    return pltpu.VMEM(shape, jnp.float32)


def first_call(at, x, g, rate, name="pre"):
    return pl.pallas_call(
        pre_kernel,
        out_shape=(f32(ROWS, 6 * SUBLANES, LANES), f32(HALF, LANES), f32(SUBLANES, LANES), f32(LANES, LANES)),
        in_specs=[pl.BlockSpec(memory_space=pltpu.SMEM)] + [pl.BlockSpec(memory_space=pltpu.HBM)] * 3,
        out_specs=tuple(vmem(4)),
        scratch_shapes=[
            pltpu.VMEM((CHANNELS, CHUNK), jnp.bfloat16),
            pltpu.VMEM((CHANNELS, CHUNK), jnp.bfloat16),
            scratch(POLES, CHANNELS),
            scratch(HALF, LANES),
            scratch(6, POLES, LANES),
            pltpu.SemaphoreType.DMA((3,)),
        ],
        compiler_params=GRANT,
        name=name,
    )(at, x, g, rate)


def body(inputs, grad_out, decay_rates, residues):
    rate = decay_rates.T
    residue = residues.T
    at = lax.axis_index("context").astype(jnp.int32).reshape(1)
    rows = [[y * ROWS + z for z in ROW_ORDER] for y in range(ROWS)]
    columns = [[y * ROWS + z for y in COLUMN_ORDER] for z in range(ROWS)]
    smem = [pl.BlockSpec(memory_space=pltpu.SMEM)]

    message, turned, packed, entry = first_call(
        at, *(pltpu.with_memory_space_constraint(v, pltpu.HBM) for v in (inputs, grad_out, rate))
    )
    received = lax.all_to_all(message, "context", 0, 0, axis_index_groups=rows, tiled=True)
    message, arrived = pl.pallas_call(
        row_kernel,
        out_shape=(f32(ROWS, 6 * SUBLANES, LANES), f32(SUBLANES, LANES)),
        in_specs=smem + vmem(2),
        out_specs=tuple(vmem(2)),
        compiler_params=GRANT,
        name="row",
    )(at, received, packed)
    received = lax.all_to_all(message, "context", 0, 0, axis_index_groups=columns, tiled=True)
    message, state = pl.pallas_call(
        column_kernel,
        out_shape=(f32(GROUP, 2 * SUBLANES, LANES), f32(SUBLANES, LANES)),
        in_specs=smem + vmem(3),
        out_specs=tuple(vmem(2)),
        compiler_params=GRANT,
        name="column",
    )(at, received, packed, arrived)
    received = lax.all_to_all(message, "channel", 0, 0, axis_index_groups=[CHANNEL_ORDER], tiled=True)

    received, rate, residue = lax.optimization_barrier((received, rate, residue))
    gain = jnp.sqrt(-jnp.expm1(-2.0 * rate))
    decay = jnp.exp(-rate)
    norm = 1.0 / math.sqrt(CHUNK * ROWS * ROWS * GROUP)
    scaled = residue * rate * norm
    grad_in, res_grad, log_grad = pl.pallas_call(
        last_kernel,
        out_shape=(jax.ShapeDtypeStruct((CHANNELS, CHUNK), jnp.bfloat16), f32(POLES, CHANNELS), f32(POLES, CHANNELS)),
        in_specs=vmem(9),
        out_specs=tuple(vmem(3)),
        scratch_shapes=[scratch(HALF, LANES)],
        compiler_params=GRANT,
        name="last",
    )(turned, entry, rate, residue * gain, state, received, gain * norm, scaled * (decay * decay / gain), scaled * gain)
    return (grad_in, res_grad.T, log_grad.T)


def solution(mesh):
    return jax.shard_map(
        body,
        mesh=mesh,
        in_specs=(P("channel", "context"), P("channel", "context"), P(), P()),
        out_specs=(P("channel", "context"), P(), P()),
        check_vma=False,
    )
```
